32 devices in a mesh: pipe: 4 (over y, x), dom: 8 (over z, core).
Axes of the slice: x: 2, y: 2, z: 4, core: 2. Of those that a mesh axis runs over, the one named last changes fastest.
Arguments:
- features: bfloat16 [8192, 512], P('dom')
- w_self: bfloat16 [4, 512, 512], P('pipe'), may hold values from -0.25 to 0.25
- w_neigh: bfloat16 [4, 512, 512], P('pipe'), may hold values from -0.25 to 0.25
- biases: float32 [4, 512], P('pipe'), may hold values from -3 to 3
- gains: float32 [4, 512], P('pipe'), may hold values from 0.5 to 1.5
- send_rows: int32 [8, 4, 8, 32], P('dom'), may hold values from 0 to 255
- send_count: int32 [8, 4, 8], P('dom'), may hold values from 0 to 32, as said below
- tile_dst: int32 [8, 4, 14], P('dom'), may hold values from 0 to 1
- tile_src: int32 [8, 4, 14], P('dom'), may hold values from 0 to 15, as said below
- tile_count: int32 [8, 4], P('dom'), may hold values from 2 to 14, as said below
- tile_vals: bfloat16 [8, 4, 14, 128, 128], P('dom'), may hold values from 0 to 4, as said below
Outputs:
- embeddings: bfloat16 [4, 8192, 512], P('pipe', 'dom')
The draws below stay inside these ranges and needn't reach their ends.
Inputs may be any that keep to these rules, and one draw needn't show every extreme that they name: `send_count`: for every stretch, some partition gets 32 rows from every partition. `tile_src`: for stretch c a source block is an own block below (c + 1) * 2, or a halo block from 8 up to below 8 + (c + 1) * 2: a stretch reads only stretches up to its own. `tile_count`: every partition has a stretch with 14 tiles. `tile_vals`: nonnegative edge weights.
All inputs are finite; a program needn't handle non-finite values.
Results may differ from the reference program's by a relative error of at most 0.0051.
Values may be sent and summed in bfloat16 or wider, within the bound.
A program may use at most 64 MiB of HBM per device.

```python
import math
import jax
import jax.numpy as jnp
from jax import lax

D = 512
TILE = 128
STRETCHES = 4
CH = 256
HALO_ROWS = 256
TILES = 14
LAYERS = 4
PARTITIONS = 8
NODES_DEV = 1024
NODES = 8192
HALO = 32
LOCAL_BLOCKS = 8
SOURCES = 16


def halo_counts(key):
    key_base, key_full = jax.random.split(jax.random.fold_in(key, 11))
    base_counts = jax.random.randint(key_base, (PARTITIONS, STRETCHES, PARTITIONS), 0, HALO + 1)
    full_target = jax.random.randint(key_full, (STRETCHES,), 0, PARTITIONS)
    is_full = jnp.arange(PARTITIONS)[None, None, :] == full_target[None, :, None]
    return (jnp.where(is_full, HALO, base_counts).astype(jnp.int32), is_full)


def draw_send_count(key, part):
    return halo_counts(key)[0]


def draw_send_rows(key, part):
    key_rows = jax.random.fold_in(key, 71)
    return jax.random.randint(key_rows, (PARTITIONS, STRETCHES, PARTITIONS, HALO), 0, CH).astype(jnp.int32)


def draw_features(key, part):
    counts, is_full = halo_counts(key)
    listed = draw_send_rows(key, part)
    picked = jnp.sum(jnp.where(is_full, listed[..., 0], 0), axis=2)
    key_value, key_zero = jax.random.split(jax.random.fold_in(key, 89))
    row_ids = jnp.arange(CH)[None, None, :]
    scattered = jax.random.randint(key_zero, (PARTITIONS, STRETCHES, CH), 0, 16) == 0
    zero_rows = (row_ids == picked[:, :, None]) | scattered
    shape_all = (PARTITIONS, STRETCHES, CH, D)
    values = jax.random.truncated_normal(key_value, -6.0, 6.0, shape_all, jnp.float32)
    return jnp.where(zero_rows[..., None], 0.0, values).reshape(NODES, D).astype(jnp.float32).astype(jnp.bfloat16)


def draw_tile_count(key, part):
    key_heavy, key_light, key_forced = jax.random.split(jax.random.fold_in(key, 23), 3)
    heavy_part = jax.random.randint(key_heavy, (PARTITIONS, 1), 0, 4) == 0
    light_counts = jax.random.randint(key_light, (PARTITIONS, STRETCHES), 2, 5)
    forced = jax.random.randint(key_forced, (PARTITIONS, 1), 0, STRETCHES)
    is_forced = jnp.arange(STRETCHES)[None, :] == forced
    return jnp.where(heavy_part | is_forced, TILES, light_counts).astype(jnp.int32)


def draw_tile_src(key, part):
    key_src = jax.random.fold_in(key, 37)
    stretch_ids = jnp.arange(STRETCHES)[None, :, None]
    own_span = (stretch_ids + 1) * (CH // TILE)
    far_span = (stretch_ids + 1) * (HALO_ROWS // TILE)
    drawn = jax.random.randint(key_src, (PARTITIONS, STRETCHES, TILES), 0, own_span + far_span)
    return jnp.where(drawn < own_span, drawn, LOCAL_BLOCKS + drawn - own_span).astype(jnp.int32)


def draw_tile_vals(key, part):
    key_edge, key_weight = jax.random.split(jax.random.fold_in(key, 53))
    shape_all = (PARTITIONS, STRETCHES, TILES, TILE, TILE)
    present = jax.random.bernoulli(key_edge, 0.08, shape_all)
    edge_weight = jnp.exp(jax.random.uniform(key_weight, shape_all, jnp.float32, math.log(0.25), math.log(4.0)))
    return jnp.where(present, edge_weight, 0.0).astype(jnp.float32).astype(jnp.bfloat16)


def with_ends(entries, rng, least, top_value):
    index_at = [jax.random.randint(jax.random.fold_in(rng, axis), (), 0, length) for axis, length in enumerate(entries.shape)]
    main_axis = entries.shape.index(max(entries.shape))
    beside = index_at[:main_axis] + [(index_at[main_axis] + 1) % entries.shape[main_axis]] + index_at[main_axis + 1:]
    return entries.at[tuple(index_at)].set(least).at[tuple(beside)].set(top_value)


def level_of(own_key, extent, cuts, low, top_value):
    def one(dim, parts):
        heights = jax.random.uniform(jax.random.fold_in(jax.random.fold_in(own_key, 6), dim), (parts,), jnp.float32, low / len(cuts), top_value / len(cuts))
        return jnp.repeat(jnp.exp(heights), extent[dim] // parts).reshape((-1,) + (1,) * (len(extent) - dim - 1))

    level = one(*cuts[0])
    for cut in cuts[1:]:
        level = level * one(*cut)
    return level


def scatter_about(stream_key, shape, deviation, most, cuts=(), kind=jnp.bfloat16):
    array = jax.random.normal(stream_key, shape, jnp.float32) * deviation
    if len(cuts) > 0:
        array = level_of(stream_key, shape, cuts, -0.22, 0.18) * array
    return jnp.clip(array, min=-most, max=most).astype(kind)


def setup_inputs(seed: int = 0) -> dict:
    splits = jax.random.split(jax.random.key(seed), 12)
    return {
        "features": draw_features(jax.random.fold_in(splits[11], 71), 0),
        "w_self": scatter_about(splits[1], (LAYERS, D, D), D ** -0.5, 0.25, ((0, 4),)),
        "w_neigh": scatter_about(splits[2], (LAYERS, D, D), D ** -0.5, 0.25, ((0, 4),)),
        "biases": scatter_about(splits[3], (LAYERS, D), 0.5, 3.0, ((0, 4),), jnp.float32),
        "gains": jnp.clip(1.0 + 0.1 * jax.random.normal(splits[4], (LAYERS, D), jnp.float32), 0.5, 1.5),
        "send_rows": draw_send_rows(jax.random.fold_in(splits[11], 71), 0),
        "send_count": draw_send_count(jax.random.fold_in(splits[11], 71), 0),
        "tile_dst": with_ends(jax.random.randint(splits[7], (PARTITIONS, STRETCHES, TILES), 0, CH // TILE), jax.random.fold_in(splits[7], 1), 0, (CH // TILE) - 1).astype(jnp.int32),
        "tile_src": draw_tile_src(jax.random.fold_in(splits[11], 71), 0),
        "tile_count": draw_tile_count(jax.random.fold_in(splits[11], 71), 0),
        "tile_vals": draw_tile_vals(jax.random.fold_in(splits[11], 71), 0),
    }


def reference(features, w_self, w_neigh, biases, gains, send_rows, send_count, tile_dst, tile_src, tile_count, tile_vals):
    slot_ids = jnp.arange(HALO, dtype=jnp.int32)
    block_ids = jnp.arange(CH // TILE, dtype=jnp.int32)
    tile_ids = jnp.arange(TILES, dtype=jnp.int32)
    peer_ids = jnp.arange(PARTITIONS, dtype=jnp.int32)[:, None, None]
    stretch_ids = jnp.arange(STRETCHES, dtype=jnp.int32)[None, :, None]
    flags_all = (slot_ids[None, None, None, :] < send_count[:, :, :, None]).astype(jnp.float32)
    current = features
    results = []
    for layer_no in range(LAYERS):
        blocks = current.reshape(PARTITIONS, STRETCHES, CH, D)

        def one_part(part_no):
            row_picks = jnp.take(send_rows, part_no, axis=2)
            slot_marks = jnp.take(flags_all, part_no, axis=2)
            fetched = blocks[peer_ids, stretch_ids, row_picks]
            halo_part = (fetched.astype(jnp.float32) * slot_marks[..., None]).astype(jnp.bfloat16)
            halo_flat = jnp.transpose(halo_part, (1, 0, 2, 3)).reshape(STRETCHES * HALO_ROWS, D)
            valid_flat = jnp.transpose(slot_marks, (1, 0, 2)).reshape(STRETCHES * HALO_ROWS)
            start_row = (part_no * NODES_DEV).astype(jnp.int32)
            own_rows = lax.dynamic_slice_in_dim(current, start_row, NODES_DEV, 0)
            source_table = jnp.concatenate([own_rows, halo_flat], axis=0).reshape(SOURCES, TILE, D)
            valid_table = jnp.concatenate([jnp.ones((NODES_DEV,), jnp.float32), valid_flat]).reshape(SOURCES, TILE)
            sources = tile_src[part_no]
            targets = tile_dst[part_no]
            counts = tile_count[part_no]
            weights = tile_vals[part_no].astype(jnp.float32)
            live_tiles = (tile_ids[None, :] < counts[:, None]).astype(jnp.float32)
            chosen = source_table[sources].astype(jnp.float32)
            contrib = jnp.einsum('ctij,ctjd->ctid', weights, chosen)
            degree_part = jnp.einsum('ctij,ctj->cti', weights, valid_table[sources])
            onehot = (targets[:, :, None] == block_ids[None, None, :]).astype(jnp.float32) * live_tiles[:, :, None]
            summed = jnp.einsum('ctr,ctid->crid', onehot, contrib).reshape(NODES_DEV, D)
            degree = jnp.einsum('ctr,cti->cri', onehot, degree_part).reshape(NODES_DEV)
            neighbour = ((own_rows.astype(jnp.float32) + summed) / (1.0 + degree)[:, None]).astype(jnp.bfloat16)
            pre_norm = jnp.dot(own_rows, w_self[layer_no], preferred_element_type=jnp.float32)
            pre_norm = pre_norm + jnp.dot(neighbour, w_neigh[layer_no], preferred_element_type=jnp.float32)
            pre_norm = pre_norm + biases[layer_no]
            normed = gains[layer_no] * pre_norm * lax.rsqrt(lax.optimization_barrier(jnp.mean(pre_norm * pre_norm, axis=-1, keepdims=True)) + 1e-05)
            if layer_no < LAYERS - 1:
                normed = jnp.maximum(normed, 0.0)
            return normed.astype(jnp.bfloat16)
        current = lax.map(one_part, jnp.arange(PARTITIONS, dtype=jnp.int32)).reshape(NODES, D)
        results.append(current)
    return jnp.stack(results)
```

```python
import functools

import jax
import jax.numpy as jnp
from jax import lax
from jax.experimental import pallas as pl
from jax.experimental.pallas import tpu as pltpu
from jax.sharding import PartitionSpec as P

MESH = pl.DeviceIdType.MESH
CHUNKS = 4
GROUP = 2


def passed_along(block, axis, distance):
    devices = range(lax.axis_size(axis))
    route = [(i - distance, i) for i in devices if i - distance in devices]
    return lax.ppermute(block, axis, route)


def staged_exchange(
    features,
    w_self,
    w_neigh,
    biases,
    gains,
    send_rows,
    send_count,
    tile_dst,
    tile_src,
    tile_count,
    tile_vals,
):
    sections = lax.axis_size("pipe")
    peer_count = lax.axis_size("dom")
    section_no = lax.axis_index("pipe")
    nodes_dev, model_width = features.shape
    stretches = tile_count.shape[1]
    tile_total = tile_src.shape[2]
    tile_size = tile_vals.shape[-1]
    stretch_rows = nodes_dev // stretches
    row_blocks = stretch_rows // tile_size
    per_peer = send_rows.shape[3]
    halo_rows = peer_count * per_peer
    steps_total = stretches + sections - 1
    is_first = section_no == 0
    is_final = section_no == sections - 1
    feature_spans = features.reshape(stretches, stretch_rows, model_width)
    slot_ids = jnp.arange(per_peer, dtype=jnp.int32)
    tile_ids = jnp.arange(tile_total, dtype=jnp.int32)
    block_ids = jnp.arange(row_blocks, dtype=jnp.int32)

    def put_rows(array_in, piece, start, active):
        old_piece = lax.dynamic_slice_in_dim(array_in, start, piece.shape[0], 0)
        return lax.dynamic_update_slice_in_dim(
            array_in, jnp.where(active, piece, old_piece), start, 0
        )

    source_table = jnp.zeros((nodes_dev + stretches * halo_rows, model_width), jnp.bfloat16)
    valid_rows = jnp.concatenate(
        [jnp.ones((nodes_dev,), jnp.float32), jnp.zeros((stretches * halo_rows,), jnp.float32)]
    )
    outputs = jnp.zeros((nodes_dev, model_width), jnp.bfloat16)
    previous = jnp.zeros((stretch_rows, model_width), jnp.bfloat16)
    for step_no in range(steps_total):
        offset = step_no - section_no
        active = (offset >= 0) & (offset < stretches)
        stretch_no = jnp.clip(offset, 0, stretches - 1)
        feed_rows = feature_spans[min(step_no, stretches - 1)]
        if step_no > 0:
            arrived = passed_along(previous, "pipe", 1)
        else:
            arrived = previous
        rows_in = jnp.where(is_first, feed_rows, arrived)
        source_table = put_rows(source_table, rows_in, stretch_no * stretch_rows, active)
        row_picks = lax.dynamic_index_in_dim(send_rows[0], stretch_no, 0, keepdims=False)
        boundary_counts = lax.dynamic_index_in_dim(send_count[0], stretch_no, 0, keepdims=False)
        slot_marks = slot_ids[None, :] < boundary_counts[:, None]
        fetched = jnp.where(slot_marks[:, :, None], rows_in[row_picks], jnp.zeros((), jnp.bfloat16))
        fetched, slot_marks = (fetched, slot_marks.astype(jnp.bfloat16))
        halo_in, marks_in = (
            lax.all_to_all(fetched, "dom", split_axis=0, concat_axis=0, tiled=True),
            lax.all_to_all(slot_marks, "dom", split_axis=0, concat_axis=0, tiled=True),
        )
        aggregate_source_table = source_table
        aggregate_valid_rows = valid_rows
        halo_start = nodes_dev + stretch_no * halo_rows
        aggregate_source_table = put_rows(
            aggregate_source_table, halo_in.reshape(halo_rows, model_width), halo_start, active
        )
        aggregate_valid_rows = put_rows(
            aggregate_valid_rows,
            marks_in.reshape(halo_rows).astype(jnp.float32),
            halo_start,
            active,
        )
        counts = tile_count[0][stretch_no]
        sources = tile_src[0][stretch_no]
        targets = tile_dst[0][stretch_no]
        weights = tile_vals[0][stretch_no]
        live = tile_ids < counts
        picks = ((targets[:, None] == block_ids[None, :]) & live[:, None]).astype(jnp.bfloat16)
        placed = jnp.einsum("tr,tij->ritj", picks, weights, preferred_element_type=jnp.float32)
        dense = placed.astype(jnp.bfloat16).reshape(stretch_rows, tile_total * tile_size)
        gathered = jnp.concatenate(
            [
                lax.dynamic_slice_in_dim(
                    aggregate_source_table, sources[t] * tile_size, tile_size, 0
                )
                for t in range(tile_total)
            ],
            axis=0,
        )
        marks = (
            aggregate_valid_rows.reshape(-1, tile_size)[sources]
            .reshape(tile_total * tile_size)
            .astype(jnp.bfloat16)
        )
        add_summed = jnp.dot(dense, gathered, preferred_element_type=jnp.float32)
        add_degree = jnp.dot(dense, marks, preferred_element_type=jnp.float32)
        source_table = aggregate_source_table
        valid_rows = aggregate_valid_rows
        neighbour = (
            (rows_in.astype(jnp.float32) + add_summed) / (1.0 + add_degree)[:, None]
        ).astype(jnp.bfloat16)
        pre_norm = jnp.dot(rows_in, w_self[0], preferred_element_type=jnp.float32)
        pre_norm = (
            pre_norm
            + jnp.dot(neighbour, w_neigh[0], preferred_element_type=jnp.float32)
            + biases[0]
        )
        normed = (
            gains[0]
            * pre_norm
            * lax.rsqrt(jnp.mean(pre_norm * pre_norm, axis=-1, keepdims=True) + 1e-05)
        )
        previous = jnp.where(is_final, normed, jnp.maximum(normed, 0.0)).astype(jnp.bfloat16)
        outputs = put_rows(outputs, previous, stretch_no * stretch_rows, active)
    return outputs[None]


def layers_kernel(
    stretches,
    feat,
    w_self_hbm,
    w_neigh_hbm,
    bias_hbm,
    gain_hbm,
    listed_hbm,
    counts_hbm,
    dst_hbm,
    src_hbm,
    used_hbm,
    vals_hbm,
    out,
    h,
    staged,
    shared,
    share_out,
    halo_out,
    halo_in,
    marks_out,
    marks_in,
    vals,
    adj,
    picks,
    scales,
    sums,
    z,
    w_self,
    w_neigh,
    bias,
    gain,
    listed,
    counts,
    dst,
    src,
    used,
    h_sem,
    hop_sem,
    halo_send,
    halo_recv,
    share_sem,
    share_send,
    mark_send,
    mark_recv,
    vals_sem,
    w_sem,
    small_sem,
):
    pipes, peers = lax.axis_size("pipe"), lax.axis_size("dom")
    pipe, me = lax.axis_index("pipe"), lax.axis_index("dom")
    _, nodes, part = h.shape
    ch = nodes // stretches
    per_peer = halo_in.shape[3]
    halo = peers * per_peer
    tiles, tile = vals.shape[1:3]
    row_blocks = ch // tile
    pair = GROUP * part

    def rows(c):
        return pl.ds(c * ch, ch)

    def cols(j):
        return pl.ds(j * part, part)

    def arrived(ref, sem):
        pltpu.make_async_copy(ref, ref, sem).wait()

    def dot(a, b):
        return jnp.dot(a, b, preferred_element_type=jnp.float32)

    mine = pl.ds(pl.multiple_of(pipe * part, part), part)
    small = [
        pltpu.make_async_copy(listed_hbm, listed, small_sem.at[0]),
        pltpu.make_async_copy(counts_hbm, counts, small_sem.at[1]),
        pltpu.make_async_copy(dst_hbm, dst, small_sem.at[2]),
        pltpu.make_async_copy(src_hbm, src, small_sem.at[3]),
        pltpu.make_async_copy(used_hbm, used, small_sem.at[4]),
        pltpu.make_async_copy(bias_hbm, bias, small_sem.at[5]),
        pltpu.make_async_copy(gain_hbm, gain, small_sem.at[6]),
    ]
    share_loads = [
        pltpu.make_async_copy(feat.at[rows(c), mine], shared.at[rows(c)], share_sem.at[c])
        for c in range(stretches)
    ]
    tile_loads = [
        pltpu.make_async_copy(vals_hbm.at[0, c], vals.at[c], vals_sem.at[c])
        for c in range(stretches)
    ]
    weights = [
        pltpu.make_async_copy(w_self_hbm.at[0], w_self, w_sem.at[0]),
        pltpu.make_async_copy(w_neigh_hbm.at[0], w_neigh, w_sem.at[1]),
    ]
    for copy in small[:2] + share_loads[:1] + small[2:] + tile_loads[:1]:
        copy.start()

    @pl.when(pipe == 0)
    def _():
        for c in range(stretches):
            for j in range(CHUNKS):
                pltpu.make_async_copy(
                    feat.at[rows(c), cols(j)], h.at[j, rows(c)], h_sem.at[c, j]
                ).start()

    for copy in weights + share_loads[1:] + tile_loads[1:]:
        copy.start()

    barrier = pltpu.get_barrier_semaphore()
    everyone = pipes * peers

    def greet(k, carry):
        other = lax.rem(pipe * peers + me + k, everyone)
        pl.semaphore_signal(
            barrier, inc=1, device_id=(other // peers, lax.rem(other, peers)), device_id_type=MESH
        )
        return carry

    lax.fori_loop(1, everyone, greet, 0)
    small[0].wait()
    small[1].wait()

    slot = lax.broadcasted_iota(jnp.int32, (1, halo), 1)
    row_ids = lax.broadcasted_iota(jnp.int32, (halo, ch), 1)

    def make_pick(c):
        limit = jnp.zeros((1, halo), jnp.int32)
        for p in range(peers):
            limit = jnp.where(slot >= p * per_peer, p * per_peer + counts[0, c, p], limit)
        rows_listed = jnp.concatenate([listed[0, c, p : p + 1, :] for p in range(peers)], axis=1)
        wanted = jnp.where(slot < limit, rows_listed, -1).astype(jnp.float32)
        column = jnp.transpose(jnp.broadcast_to(wanted, (8, halo)))[:, :1].astype(jnp.int32)
        picks[c] = jnp.where(row_ids == column, 1.0, 0.0).astype(jnp.bfloat16)

    def share(c):
        share_loads[c].wait()
        sent = dot(picks[c], shared[rows(c), :])
        share_out[c] = sent.astype(jnp.bfloat16).reshape(peers, per_peer, part)

        def send(k, carry):
            to = lax.rem(me + k, peers)
            pltpu.make_async_remote_copy(
                src_ref=share_out.at[c, to],
                dst_ref=halo_in.at[c, pipe, me],
                send_sem=share_send.at[c],
                recv_sem=halo_recv.at[c, pipe],
                device_id=(0, to),
                device_id_type=MESH,
            ).start()
            return carry

        lax.fori_loop(1, peers, send, 0)

        @pl.when(pipe == 0)
        def _():
            pltpu.make_async_copy(
                share_out.at[c, me], halo_in.at[c, 0, me], halo_recv.at[c, 0]
            ).start()

        @pl.when(pipe > 0)
        def _():
            send(0, 0)

    make_pick(0)
    pl.semaphore_wait(barrier, everyone - 1)
    share(0)

    mark_shape = marks_out.shape[1:]
    mark_row = lax.broadcasted_iota(jnp.int32, mark_shape, 0)
    mark_slot = lax.broadcasted_iota(jnp.int32, mark_shape, 1) - me * per_peer
    for p in range(peers):
        limit = jnp.zeros(mark_shape, jnp.int32)
        for c in range(stretches):
            limit = jnp.where(mark_row == c, counts[0, c, p], limit)
        mark = (mark_slot >= 0) & (mark_slot < limit)
        marks_out[p] = jnp.where(mark, 1.0, 0.0).astype(jnp.bfloat16)

    def send_marks(k, carry):
        to = lax.rem(me + k, peers)
        pltpu.make_async_remote_copy(
            src_ref=marks_out.at[to],
            dst_ref=marks_in.at[me],
            send_sem=mark_send,
            recv_sem=mark_recv,
            device_id=(pipe, to),
            device_id_type=MESH,
        ).start()
        return carry

    lax.fori_loop(1, peers, send_marks, 0)
    pltpu.make_async_copy(marks_out.at[me], marks_in.at[me], mark_recv).start()

    for copy in small[2:5]:
        copy.wait()

    def build(c):
        tile_loads[c].wait()
        codes = [
            jnp.where(t < used[0, c], src[0, c, t] * row_blocks + dst[0, c, t], -1)
            for t in range(tiles)
        ]

        def blocks(first, count):
            def one(i, carry):
                b = first + i
                totals = [jnp.zeros((tile, tile), jnp.float32) for _ in range(row_blocks)]
                for t in range(tiles):
                    weight = vals[c, t].astype(jnp.float32)
                    for r in range(row_blocks):
                        on = jnp.where(codes[t] == b * row_blocks + r, 1.0, 0.0)
                        totals[r] = totals[r] + weight * on
                at = pl.ds(pl.multiple_of(b * tile, tile), tile)
                for r in range(row_blocks):
                    adj[c, r * tile : (r + 1) * tile, at] = totals[r].astype(jnp.bfloat16)
                return carry

            lax.fori_loop(0, count, one, 0)

        blocks(0, (c + 1) * ch // tile)
        blocks(nodes // tile, (c + 1) * halo // tile)

    over_rows = (((1,), (1,)), ((), ()))

    def far(c, d):
        return adj[c, :, nodes + d * halo : nodes + (d + 1) * halo]

    def make_scale(c):
        own = (c + 1) * ch
        valid = marks_in[0]
        for q in range(1, peers):
            valid = valid + marks_in[q]
        ones = jnp.ones((valid.shape[0], own), jnp.bfloat16)
        deg = lax.dot_general(
            adj[c, :, :own], ones, over_rows, preferred_element_type=jnp.float32
        )[:, :1]
        for d in range(c + 1):
            deg = deg + lax.dot_general(
                far(c, d), valid, over_rows, preferred_element_type=jnp.float32
            )[:, d : d + 1]
        scales[c] = jnp.broadcast_to(1.0 / (1.0 + deg), (ch, part))

    def send_chunk(c, j):
        arrived(h.at[j, rows(c)], h_sem.at[c, j])
        sent = dot(picks[c], h[j, rows(c), :])
        halo_out[c, j] = sent.astype(jnp.bfloat16).reshape(peers, per_peer, part)

        def send(k, carry):
            to = lax.rem(me + k, peers)
            pltpu.make_async_remote_copy(
                src_ref=halo_out.at[c, j, to],
                dst_ref=halo_in.at[c, j, me],
                send_sem=halo_send.at[c, j],
                recv_sem=halo_recv.at[c, j],
                device_id=(pipe, to),
                device_id_type=MESH,
            ).start()
            return carry

        lax.fori_loop(1, peers, send, 0)
        pltpu.make_async_copy(
            halo_out.at[c, j, me], halo_in.at[c, j, me], halo_recv.at[c, j]
        ).start()

    def near_sums(c):
        own = (c + 1) * ch
        total = bias[...]
        for g in range(CHUNKS // GROUP):
            js = range(g * GROUP, (g + 1) * GROUP)
            held = jnp.concatenate([h[j, rows(c), :] for j in js], axis=1)
            total = total + dot(held, w_self[pl.ds(g * pair, pair), :])
            added = held.astype(jnp.float32) + dot(
                adj[c, :, :own], jnp.concatenate([h[j, :own, :] for j in js], axis=1)
            )
            for d in range(c):
                added = added + dot(
                    far(c, d),
                    jnp.concatenate([halo_in[d, j].reshape(halo, part) for j in js], axis=1),
                )
            sums[:, pl.ds(g * pair, pair)] = added
        z[...] = total

    def far_sums(c, js):
        for j in js:
            arrived(halo_in.at[c, j], halo_recv.at[c, j])
        fetched = jnp.concatenate([halo_in[c, j].reshape(halo, part) for j in js], axis=1)
        span = pl.ds(js[0] * part, len(js) * part)
        scale = jnp.concatenate([scales[c]] * len(js), axis=1)
        agg = (sums[:, span] + dot(far(c, c), fetched)) * scale
        z[...] += dot(agg.astype(jnp.bfloat16), w_neigh[span, :])

    floor = jnp.where(pipe == pipes - 1, -jnp.inf, 0.0).astype(jnp.float32)

    def finish(c):
        value = z[...]
        u = gain[...] * value * lax.rsqrt(jnp.mean(value * value, axis=-1, keepdims=True) + 1e-05)
        result = jnp.maximum(u, floor).astype(jnp.bfloat16)

        @pl.when(pipe < pipes - 1)
        def _():
            for j in range(CHUNKS):
                staged[j, rows(c), :] = result[:, j * part : (j + 1) * part]
                pltpu.make_async_remote_copy(
                    src_ref=staged.at[j, rows(c)],
                    dst_ref=h.at[j, rows(c)],
                    send_sem=hop_sem.at[c, j],
                    recv_sem=h_sem.at[c, j],
                    device_id=(pipe + 1, me),
                    device_id_type=MESH,
                ).start()

        out[rows(c), :] = result

    def wait_weights():
        for copy in weights + small[5:]:
            copy.wait()

    build(0)

    @pl.when(pipe == 0)
    def _():
        make_pick(1)
        share(1)
        arrived(marks_in, mark_recv)
        make_scale(0)
        wait_weights()
        for c in range(stretches):
            if c > 0:
                build(c)
                make_scale(c)
            for j in range(CHUNKS):
                arrived(h.at[j, rows(c)], h_sem.at[c, j])
            near_sums(c)
            if 0 < c < stretches - 1:
                make_pick(c + 1)
                share(c + 1)
            far_sums(c, (0, 1))
            far_sums(c, (2,))
            far_sums(c, (3,))
            finish(c)

    @pl.when(pipe > 0)
    def _():
        for c in range(1, stretches):
            make_pick(c)
            share(c)
            build(c)
        arrived(marks_in, mark_recv)
        for c in range(stretches):
            make_scale(c)
        wait_weights()
        for j in range(CHUNKS):
            send_chunk(0, j)
        for c in range(stretches):
            more = c + 1 < stretches
            near_sums(c)
            far_sums(c, (0, 1))
            if more:
                send_chunk(c + 1, 0)
            far_sums(c, (2,))
            if more:
                send_chunk(c + 1, 1)
            far_sums(c, (3,))
            finish(c)
            if more:
                send_chunk(c + 1, 2)
                send_chunk(c + 1, 3)

    others = pl.ds(0, peers - 1)
    arrived(marks_out.at[others], mark_send)

    @pl.when(pipe == 0)
    def _():
        for c in range(stretches):
            arrived(share_out.at[c, others], share_send.at[c])

    @pl.when(pipe > 0)
    def _():
        for c in range(stretches):
            arrived(share_out.at[c], share_send.at[c])
            for j in range(CHUNKS):
                arrived(halo_out.at[c, j, others], halo_send.at[c, j])

    @pl.when(pipe < pipes - 1)
    def _():
        for c in range(stretches):
            for j in range(CHUNKS):
                arrived(staged.at[j, rows(c)], hop_sem.at[c, j])


def pipelined(
    features,
    w_self,
    w_neigh,
    biases,
    gains,
    send_rows,
    send_count,
    tile_dst,
    tile_src,
    tile_count,
    tile_vals,
):
    peers = lax.axis_size("dom")
    nodes, width = features.shape
    stretches = tile_count.shape[1]
    per_peer = send_rows.shape[3]
    ch = nodes // stretches
    halo = peers * per_peer
    part = width // CHUNKS
    sources = nodes + stretches * halo
    tiles = tile_vals.shape[1:]
    anywhere = pl.BlockSpec(memory_space=pl.ANY)
    halo_shape = (stretches, CHUNKS, peers, per_peer, part)
    out = pl.pallas_call(
        functools.partial(layers_kernel, stretches),
        out_shape=jax.ShapeDtypeStruct((nodes, width), jnp.bfloat16),
        in_specs=[anywhere] * 11,
        out_specs=pl.BlockSpec(memory_space=pltpu.VMEM),
        scratch_shapes=[
            pltpu.VMEM((CHUNKS, nodes, part), jnp.bfloat16),
            pltpu.VMEM((CHUNKS, nodes, part), jnp.bfloat16),
            pltpu.VMEM((nodes, part), jnp.bfloat16),
            pltpu.VMEM((stretches, peers, per_peer, part), jnp.bfloat16),
            pltpu.VMEM(halo_shape, jnp.bfloat16),
            pltpu.VMEM(halo_shape, jnp.bfloat16),
            pltpu.VMEM((peers, 8, halo), jnp.bfloat16),
            pltpu.VMEM((peers, 8, halo), jnp.bfloat16),
            pltpu.VMEM(tiles, jnp.bfloat16),
            pltpu.VMEM((stretches, ch, sources), jnp.bfloat16),
            pltpu.VMEM((stretches, halo, ch), jnp.bfloat16),
            pltpu.VMEM((stretches, ch, part), jnp.float32),
            pltpu.VMEM((ch, width), jnp.float32),
            pltpu.VMEM((ch, width), jnp.float32),
            pltpu.VMEM((width, width), jnp.bfloat16),
            pltpu.VMEM((width, width), jnp.bfloat16),
            pltpu.VMEM(biases.shape, jnp.float32),
            pltpu.VMEM(gains.shape, jnp.float32),
            pltpu.VMEM(send_rows.shape, jnp.int32),
            pltpu.SMEM(send_count.shape, jnp.int32),
            pltpu.SMEM(tile_dst.shape, jnp.int32),
            pltpu.SMEM(tile_src.shape, jnp.int32),
            pltpu.SMEM(tile_count.shape, jnp.int32),
            pltpu.SemaphoreType.DMA((stretches, CHUNKS)),
            pltpu.SemaphoreType.DMA((stretches, CHUNKS)),
            pltpu.SemaphoreType.DMA((stretches, CHUNKS)),
            pltpu.SemaphoreType.DMA((stretches, CHUNKS)),
            pltpu.SemaphoreType.DMA((stretches,)),
            pltpu.SemaphoreType.DMA((stretches,)),
            pltpu.SemaphoreType.DMA,
            pltpu.SemaphoreType.DMA,
            pltpu.SemaphoreType.DMA((stretches,)),
            pltpu.SemaphoreType.DMA((2,)),
            pltpu.SemaphoreType.DMA((7,)),
        ],
        compiler_params=pltpu.CompilerParams(
            collective_id=0, has_side_effects=True, vmem_limit_bytes=56 * 2**20
        ),
        name="layers",
    )(
        features,
        w_self,
        w_neigh,
        biases,
        gains,
        send_rows,
        send_count,
        tile_dst,
        tile_src,
        tile_count,
        tile_vals,
    )
    return out[None]


def on_device(*args):
    send_rows, tile_vals = args[5], args[10]
    per_peer, tile = send_rows.shape[3], tile_vals.shape[-1]
    if per_peer % 16 or tile != 128 or args[9].shape[1] > 8 or lax.axis_size("pipe") != CHUNKS:
        return staged_exchange(*args)
    return pipelined(*args)


def solution(mesh):
    placed = (
        P("dom", None),
        P("pipe", None, None),
        P("pipe", None, None),
        P("pipe", None),
        P("pipe", None),
        P("dom", None, None, None),
        P("dom", None, None),
        P("dom", None, None),
        P("dom", None, None),
        P("dom", None),
        P("dom", None, None, None, None),
    )
    return jax.shard_map(
        on_device, mesh=mesh, in_specs=placed, out_specs=P("pipe", "dom", None), check_vma=False
    )
```

```python
import functools

import jax
import jax.numpy as jnp
from jax import lax
from jax.experimental import pallas as pl
from jax.experimental.pallas import tpu as pltpu
from jax.sharding import PartitionSpec as P

MESH = pl.DeviceIdType.MESH
CHUNKS = 4
GROUP = 2
LEAD = 3


def passed_along(block, axis, distance):
    devices = range(lax.axis_size(axis))
    route = [(i - distance, i) for i in devices if i - distance in devices]
    return lax.ppermute(block, axis, route)


def staged_exchange(
    features,
    w_self,
    w_neigh,
    biases,
    gains,
    send_rows,
    send_count,
    tile_dst,
    tile_src,
    tile_count,
    tile_vals,
):
    sections = lax.axis_size("pipe")
    peer_count = lax.axis_size("dom")
    section_no = lax.axis_index("pipe")
    nodes_dev, model_width = features.shape
    stretches = tile_count.shape[1]
    tile_total = tile_src.shape[2]
    tile_size = tile_vals.shape[-1]
    stretch_rows = nodes_dev // stretches
    row_blocks = stretch_rows // tile_size
    per_peer = send_rows.shape[3]
    halo_rows = peer_count * per_peer
    steps_total = stretches + sections - 1
    is_first = section_no == 0
    is_final = section_no == sections - 1
    feature_spans = features.reshape(stretches, stretch_rows, model_width)
    slot_ids = jnp.arange(per_peer, dtype=jnp.int32)
    tile_ids = jnp.arange(tile_total, dtype=jnp.int32)
    block_ids = jnp.arange(row_blocks, dtype=jnp.int32)

    def put_rows(array_in, piece, start, active):
        old_piece = lax.dynamic_slice_in_dim(array_in, start, piece.shape[0], 0)
        return lax.dynamic_update_slice_in_dim(
            array_in, jnp.where(active, piece, old_piece), start, 0
        )

    source_table = jnp.zeros((nodes_dev + stretches * halo_rows, model_width), jnp.bfloat16)
    valid_rows = jnp.concatenate(
        [jnp.ones((nodes_dev,), jnp.float32), jnp.zeros((stretches * halo_rows,), jnp.float32)]
    )
    outputs = jnp.zeros((nodes_dev, model_width), jnp.bfloat16)
    previous = jnp.zeros((stretch_rows, model_width), jnp.bfloat16)
    for step_no in range(steps_total):
        offset = step_no - section_no
        active = (offset >= 0) & (offset < stretches)
        stretch_no = jnp.clip(offset, 0, stretches - 1)
        feed_rows = feature_spans[min(step_no, stretches - 1)]
        if step_no > 0:
            arrived = passed_along(previous, "pipe", 1)
        else:
            arrived = previous
        rows_in = jnp.where(is_first, feed_rows, arrived)
        source_table = put_rows(source_table, rows_in, stretch_no * stretch_rows, active)
        row_picks = lax.dynamic_index_in_dim(send_rows[0], stretch_no, 0, keepdims=False)
        boundary_counts = lax.dynamic_index_in_dim(send_count[0], stretch_no, 0, keepdims=False)
        slot_marks = slot_ids[None, :] < boundary_counts[:, None]
        fetched = jnp.where(slot_marks[:, :, None], rows_in[row_picks], jnp.zeros((), jnp.bfloat16))
        fetched, slot_marks = (fetched, slot_marks.astype(jnp.bfloat16))
        halo_in, marks_in = (
            lax.all_to_all(fetched, "dom", split_axis=0, concat_axis=0, tiled=True),
            lax.all_to_all(slot_marks, "dom", split_axis=0, concat_axis=0, tiled=True),
        )
        aggregate_source_table = source_table
        aggregate_valid_rows = valid_rows
        halo_start = nodes_dev + stretch_no * halo_rows
        aggregate_source_table = put_rows(
            aggregate_source_table, halo_in.reshape(halo_rows, model_width), halo_start, active
        )
        aggregate_valid_rows = put_rows(
            aggregate_valid_rows,
            marks_in.reshape(halo_rows).astype(jnp.float32),
            halo_start,
            active,
        )
        counts = tile_count[0][stretch_no]
        sources = tile_src[0][stretch_no]
        targets = tile_dst[0][stretch_no]
        weights = tile_vals[0][stretch_no]
        live = tile_ids < counts
        picks = ((targets[:, None] == block_ids[None, :]) & live[:, None]).astype(jnp.bfloat16)
        placed = jnp.einsum("tr,tij->ritj", picks, weights, preferred_element_type=jnp.float32)
        dense = placed.astype(jnp.bfloat16).reshape(stretch_rows, tile_total * tile_size)
        gathered = jnp.concatenate(
            [
                lax.dynamic_slice_in_dim(
                    aggregate_source_table, sources[t] * tile_size, tile_size, 0
                )
                for t in range(tile_total)
            ],
            axis=0,
        )
        marks = (
            aggregate_valid_rows.reshape(-1, tile_size)[sources]
            .reshape(tile_total * tile_size)
            .astype(jnp.bfloat16)
        )
        add_summed = jnp.dot(dense, gathered, preferred_element_type=jnp.float32)
        add_degree = jnp.dot(dense, marks, preferred_element_type=jnp.float32)
        source_table = aggregate_source_table
        valid_rows = aggregate_valid_rows
        neighbour = (
            (rows_in.astype(jnp.float32) + add_summed) / (1.0 + add_degree)[:, None]
        ).astype(jnp.bfloat16)
        pre_norm = jnp.dot(rows_in, w_self[0], preferred_element_type=jnp.float32)
        pre_norm = (
            pre_norm
            + jnp.dot(neighbour, w_neigh[0], preferred_element_type=jnp.float32)
            + biases[0]
        )
        normed = (
            gains[0]
            * pre_norm
            * lax.rsqrt(jnp.mean(pre_norm * pre_norm, axis=-1, keepdims=True) + 1e-05)
        )
        previous = jnp.where(is_final, normed, jnp.maximum(normed, 0.0)).astype(jnp.bfloat16)
        outputs = put_rows(outputs, previous, stretch_no * stretch_rows, active)
    return outputs[None]


def layers_kernel(
    stretches,
    feat,
    w_self_hbm,
    w_neigh_hbm,
    bias_hbm,
    gain_hbm,
    listed_hbm,
    counts_hbm,
    dst_hbm,
    src_hbm,
    used_hbm,
    vals_hbm,
    out,
    h,
    staged,
    shared,
    share_out,
    halo_out,
    halo_in,
    marks_out,
    marks_in,
    vals,
    adj,
    picks,
    scales,
    sums,
    z,
    w_self,
    w_neigh,
    bias,
    gain,
    listed,
    counts,
    dst,
    src,
    used,
    h_sem,
    hop_sem,
    halo_send,
    halo_recv,
    share_sem,
    share_send,
    mark_send,
    mark_recv,
    vals_sem,
    w_sem,
    small_sem,
):
    pipes, peers = lax.axis_size("pipe"), lax.axis_size("dom")
    pipe, me = lax.axis_index("pipe"), lax.axis_index("dom")
    _, nodes, part = h.shape
    ch = nodes // stretches
    per_peer = halo_in.shape[3]
    halo = peers * per_peer
    tiles, tile = vals.shape[1:3]
    row_blocks = ch // tile
    pair = GROUP * part

    def rows(c):
        return pl.ds(c * ch, ch)

    def cols(j):
        return pl.ds(j * part, part)

    def arrived(ref, sem):
        pltpu.make_async_copy(ref, ref, sem).wait()

    def dot(a, b):
        return jnp.dot(a, b, preferred_element_type=jnp.float32)

    mine = pl.ds(pl.multiple_of(pipe * part, part), part)
    small = [
        pltpu.make_async_copy(listed_hbm, listed, small_sem.at[0]),
        pltpu.make_async_copy(counts_hbm, counts, small_sem.at[1]),
        pltpu.make_async_copy(dst_hbm, dst, small_sem.at[2]),
        pltpu.make_async_copy(src_hbm, src, small_sem.at[3]),
        pltpu.make_async_copy(used_hbm, used, small_sem.at[4]),
        pltpu.make_async_copy(bias_hbm, bias, small_sem.at[5]),
        pltpu.make_async_copy(gain_hbm, gain, small_sem.at[6]),
    ]
    share_loads = [
        pltpu.make_async_copy(feat.at[rows(c), mine], shared.at[rows(c)], share_sem.at[c])
        for c in range(stretches)
    ]
    tile_loads = [
        pltpu.make_async_copy(vals_hbm.at[0, c], vals.at[c], vals_sem.at[c])
        for c in range(stretches)
    ]
    weights = [
        pltpu.make_async_copy(w_self_hbm.at[0], w_self, w_sem.at[0]),
        pltpu.make_async_copy(w_neigh_hbm.at[0], w_neigh, w_sem.at[1]),
    ]
    for copy in small[:2] + share_loads[:1] + small[2:] + tile_loads[:1]:
        copy.start()

    @pl.when(pipe == 0)
    def _():
        for c in range(stretches):
            for j in range(CHUNKS):
                pltpu.make_async_copy(
                    feat.at[rows(c), cols(j)], h.at[j, rows(c)], h_sem.at[c, j]
                ).start()

    for copy in weights + share_loads[1:] + tile_loads[1:]:
        copy.start()

    barrier = pltpu.get_barrier_semaphore()
    everyone = pipes * peers

    def greet(k, carry):
        other = lax.rem(pipe * peers + me + k, everyone)
        pl.semaphore_signal(
            barrier, inc=1, device_id=(other // peers, lax.rem(other, peers)), device_id_type=MESH
        )
        return carry

    lax.fori_loop(1, everyone, greet, 0)
    small[0].wait()
    small[1].wait()

    slot = lax.broadcasted_iota(jnp.int32, (1, halo), 1)
    row_ids = lax.broadcasted_iota(jnp.int32, (halo, ch), 1)

    def make_pick(c):
        limit = jnp.zeros((1, halo), jnp.int32)
        for p in range(peers):
            limit = jnp.where(slot >= p * per_peer, p * per_peer + counts[0, c, p], limit)
        rows_listed = jnp.concatenate([listed[0, c, p : p + 1, :] for p in range(peers)], axis=1)
        wanted = jnp.where(slot < limit, rows_listed, -1).astype(jnp.float32)
        column = jnp.transpose(jnp.broadcast_to(wanted, (8, halo)))[:, :1].astype(jnp.int32)
        picks[c] = jnp.where(row_ids == column, 1.0, 0.0).astype(jnp.bfloat16)

    def share(c):
        share_loads[c].wait()
        sent = dot(picks[c], shared[rows(c), :])
        share_out[c] = sent.astype(jnp.bfloat16).reshape(peers, per_peer, part)

        def send(k, carry):
            to = lax.rem(me + k, peers)
            pltpu.make_async_remote_copy(
                src_ref=share_out.at[c, to],
                dst_ref=halo_in.at[c, pipe, me],
                send_sem=share_send.at[c],
                recv_sem=halo_recv.at[c, pipe],
                device_id=(0, to),
                device_id_type=MESH,
            ).start()
            return carry

        lax.fori_loop(1, peers, send, 0)

        @pl.when(pipe == 0)
        def _():
            pltpu.make_async_copy(
                share_out.at[c, me], halo_in.at[c, 0, me], halo_recv.at[c, 0]
            ).start()

        @pl.when(pipe > 0)
        def _():
            send(0, 0)

    make_pick(0)
    pl.semaphore_wait(barrier, everyone - 1)
    share(0)

    mark_shape = marks_out.shape[1:]
    mark_row = lax.broadcasted_iota(jnp.int32, mark_shape, 0)
    mark_slot = lax.broadcasted_iota(jnp.int32, mark_shape, 1) - me * per_peer
    for p in range(peers):
        limit = jnp.zeros(mark_shape, jnp.int32)
        for c in range(stretches):
            limit = jnp.where(mark_row == c, counts[0, c, p], limit)
        mark = (mark_slot >= 0) & (mark_slot < limit)
        marks_out[p] = jnp.where(mark, 1.0, 0.0).astype(jnp.bfloat16)

    def send_marks(k, carry):
        to = lax.rem(me + k, peers)
        pltpu.make_async_remote_copy(
            src_ref=marks_out.at[to],
            dst_ref=marks_in.at[me],
            send_sem=mark_send,
            recv_sem=mark_recv,
            device_id=(pipe, to),
            device_id_type=MESH,
        ).start()
        return carry

    lax.fori_loop(1, peers, send_marks, 0)
    pltpu.make_async_copy(marks_out.at[me], marks_in.at[me], mark_recv).start()

    for copy in small[2:5]:
        copy.wait()

    def build(c):
        tile_loads[c].wait()
        codes = [
            jnp.where(t < used[0, c], src[0, c, t] * row_blocks + dst[0, c, t], -1)
            for t in range(tiles)
        ]

        def blocks(first, count):
            def one(i, carry):
                b = first + i
                totals = [jnp.zeros((tile, tile), jnp.float32) for _ in range(row_blocks)]
                for t in range(tiles):
                    weight = vals[c, t].astype(jnp.float32)
                    for r in range(row_blocks):
                        on = jnp.where(codes[t] == b * row_blocks + r, 1.0, 0.0)
                        totals[r] = totals[r] + weight * on
                at = pl.ds(pl.multiple_of(b * tile, tile), tile)
                for r in range(row_blocks):
                    adj[c, r * tile : (r + 1) * tile, at] = totals[r].astype(jnp.bfloat16)
                return carry

            lax.fori_loop(0, count, one, 0)

        blocks(0, (c + 1) * ch // tile)
        blocks(nodes // tile, (c + 1) * halo // tile)

    over_rows = (((1,), (1,)), ((), ()))

    def far(c, d):
        return adj[c, :, nodes + d * halo : nodes + (d + 1) * halo]

    def make_scale(c):
        own = (c + 1) * ch
        valid = marks_in[0]
        for q in range(1, peers):
            valid = valid + marks_in[q]
        ones = jnp.ones((valid.shape[0], own), jnp.bfloat16)
        deg = lax.dot_general(
            adj[c, :, :own], ones, over_rows, preferred_element_type=jnp.float32
        )[:, :1]
        for d in range(c + 1):
            deg = deg + lax.dot_general(
                far(c, d), valid, over_rows, preferred_element_type=jnp.float32
            )[:, d : d + 1]
        scales[c] = jnp.broadcast_to(1.0 / (1.0 + deg), (ch, part))

    def send_chunk(c, j):
        arrived(h.at[j, rows(c)], h_sem.at[c, j])
        sent = dot(picks[c], h[j, rows(c), :])
        halo_out[c, j] = sent.astype(jnp.bfloat16).reshape(peers, per_peer, part)

        def send(k, carry):
            to = lax.rem(me + k, peers)
            pltpu.make_async_remote_copy(
                src_ref=halo_out.at[c, j, to],
                dst_ref=halo_in.at[c, j, me],
                send_sem=halo_send.at[c, j],
                recv_sem=halo_recv.at[c, j],
                device_id=(pipe, to),
                device_id_type=MESH,
            ).start()
            return carry

        lax.fori_loop(1, peers, send, 0)
        pltpu.make_async_copy(
            halo_out.at[c, j, me], halo_in.at[c, j, me], halo_recv.at[c, j]
        ).start()

    def near_sums(c):
        own = (c + 1) * ch
        total = bias[...]
        for g in range(CHUNKS // GROUP):
            js = range(g * GROUP, (g + 1) * GROUP)
            held = jnp.concatenate([h[j, rows(c), :] for j in js], axis=1)
            total = total + dot(held, w_self[pl.ds(g * pair, pair), :])
            added = held.astype(jnp.float32) + dot(
                adj[c, :, :own], jnp.concatenate([h[j, :own, :] for j in js], axis=1)
            )
            for d in range(c):
                added = added + dot(
                    far(c, d),
                    jnp.concatenate([halo_in[d, j].reshape(halo, part) for j in js], axis=1),
                )
            sums[:, pl.ds(g * pair, pair)] = added
        z[...] = total

    def far_sums(c, js):
        for j in js:
            arrived(halo_in.at[c, j], halo_recv.at[c, j])
        fetched = jnp.concatenate([halo_in[c, j].reshape(halo, part) for j in js], axis=1)
        span = pl.ds(js[0] * part, len(js) * part)
        scale = jnp.concatenate([scales[c]] * len(js), axis=1)
        agg = (sums[:, span] + dot(far(c, c), fetched)) * scale
        z[...] += dot(agg.astype(jnp.bfloat16), w_neigh[span, :])

    floor = jnp.where(pipe == pipes - 1, -jnp.inf, 0.0).astype(jnp.float32)

    def finish(c):
        value = z[...]
        u = gain[...] * value * lax.rsqrt(jnp.mean(value * value, axis=-1, keepdims=True) + 1e-05)
        result = jnp.maximum(u, floor).astype(jnp.bfloat16)

        @pl.when(pipe < pipes - 1)
        def _():
            for j in range(CHUNKS):
                staged[j, rows(c), :] = result[:, j * part : (j + 1) * part]
                pltpu.make_async_remote_copy(
                    src_ref=staged.at[j, rows(c)],
                    dst_ref=h.at[j, rows(c)],
                    send_sem=hop_sem.at[c, j],
                    recv_sem=h_sem.at[c, j],
                    device_id=(pipe + 1, me),
                    device_id_type=MESH,
                ).start()

        out[rows(c), :] = result

    def wait_weights():
        for copy in weights + small[5:]:
            copy.wait()

    build(0)

    @pl.when(pipe == 0)
    def _():
        for c in range(stretches):
            for j in range(CHUNKS):
                arrived(h.at[j, rows(c)], h_sem.at[c, j])
            if c == 0:
                wait_weights()
            near_sums(c)
            if c + 1 < stretches:
                make_pick(c + 1)
                share(c + 1)
            if c == 0:
                arrived(marks_in, mark_recv)
            make_scale(c)
            for j in range(CHUNKS):
                far_sums(c, (j,))
            finish(c)
            if c + 1 < stretches:
                build(c + 1)

    @pl.when(pipe > 0)
    def _():
        for c in range(1, stretches):
            build(c)
            make_pick(c)
            share(c)
        arrived(marks_in, mark_recv)
        for c in range(stretches):
            make_scale(c)
        wait_weights()
        for j in range(CHUNKS):
            send_chunk(0, j)
        for c in range(stretches):
            near_sums(c)
            for j in range(CHUNKS):
                if c + 1 < stretches and 0 < j <= LEAD:
                    send_chunk(c + 1, j - 1)
                far_sums(c, (j,))
            finish(c)
            if c + 1 < stretches:
                for j in range(min(LEAD, CHUNKS - 1), CHUNKS):
                    send_chunk(c + 1, j)

    others = pl.ds(0, peers - 1)
    arrived(marks_out.at[others], mark_send)

    @pl.when(pipe == 0)
    def _():
        for c in range(stretches):
            arrived(share_out.at[c, others], share_send.at[c])

    @pl.when(pipe > 0)
    def _():
        for c in range(stretches):
            arrived(share_out.at[c], share_send.at[c])
            for j in range(CHUNKS):
                arrived(halo_out.at[c, j, others], halo_send.at[c, j])

    @pl.when(pipe < pipes - 1)
    def _():
        for c in range(stretches):
            for j in range(CHUNKS):
                arrived(staged.at[j, rows(c)], hop_sem.at[c, j])


def pipelined(
    features,
    w_self,
    w_neigh,
    biases,
    gains,
    send_rows,
    send_count,
    tile_dst,
    tile_src,
    tile_count,
    tile_vals,
):
    peers = lax.axis_size("dom")
    nodes, width = features.shape
    stretches = tile_count.shape[1]
    per_peer = send_rows.shape[3]
    ch = nodes // stretches
    halo = peers * per_peer
    part = width // CHUNKS
    sources = nodes + stretches * halo
    tiles = tile_vals.shape[1:]
    anywhere = pl.BlockSpec(memory_space=pltpu.HBM)
    halo_shape = (stretches, CHUNKS, peers, per_peer, part)
    out = pl.pallas_call(
        functools.partial(layers_kernel, stretches),
        out_shape=pltpu.VMEM((nodes, width), jnp.bfloat16),
        in_specs=[anywhere] * 11,
        out_specs=pl.BlockSpec(memory_space=pltpu.VMEM),
        scratch_shapes=[
            pltpu.VMEM((CHUNKS, nodes, part), jnp.bfloat16),
            pltpu.VMEM((CHUNKS, nodes, part), jnp.bfloat16),
            pltpu.VMEM((nodes, part), jnp.bfloat16),
            pltpu.VMEM((stretches, peers, per_peer, part), jnp.bfloat16),
            pltpu.VMEM(halo_shape, jnp.bfloat16),
            pltpu.VMEM(halo_shape, jnp.bfloat16),
            pltpu.VMEM((peers, 8, halo), jnp.bfloat16),
            pltpu.VMEM((peers, 8, halo), jnp.bfloat16),
            pltpu.VMEM(tiles, jnp.bfloat16),
            pltpu.VMEM((stretches, ch, sources), jnp.bfloat16),
            pltpu.VMEM((stretches, halo, ch), jnp.bfloat16),
            pltpu.VMEM((stretches, ch, part), jnp.float32),
            pltpu.VMEM((ch, width), jnp.float32),
            pltpu.VMEM((ch, width), jnp.float32),
            pltpu.VMEM((width, width), jnp.bfloat16),
            pltpu.VMEM((width, width), jnp.bfloat16),
            pltpu.VMEM(biases.shape, jnp.float32),
            pltpu.VMEM(gains.shape, jnp.float32),
            pltpu.VMEM(send_rows.shape, jnp.int32),
            pltpu.SMEM(send_count.shape, jnp.int32),
            pltpu.SMEM(tile_dst.shape, jnp.int32),
            pltpu.SMEM(tile_src.shape, jnp.int32),
            pltpu.SMEM(tile_count.shape, jnp.int32),
            pltpu.SemaphoreType.DMA((stretches, CHUNKS)),
            pltpu.SemaphoreType.DMA((stretches, CHUNKS)),
            pltpu.SemaphoreType.DMA((stretches, CHUNKS)),
            pltpu.SemaphoreType.DMA((stretches, CHUNKS)),
            pltpu.SemaphoreType.DMA((stretches,)),
            pltpu.SemaphoreType.DMA((stretches,)),
            pltpu.SemaphoreType.DMA,
            pltpu.SemaphoreType.DMA,
            pltpu.SemaphoreType.DMA((stretches,)),
            pltpu.SemaphoreType.DMA((2,)),
            pltpu.SemaphoreType.DMA((7,)),
        ],
        compiler_params=pltpu.CompilerParams(
            collective_id=0, has_side_effects=True, vmem_limit_bytes=40 * 2**20
        ),
        name="layers",
    )(
        *(
            pltpu.with_memory_space_constraint(array, pltpu.HBM)
            for array in (
                features,
                w_self,
                w_neigh,
                biases,
                gains,
                send_rows,
                send_count,
                tile_dst,
                tile_src,
                tile_count,
                tile_vals,
            )
        )
    )
    return out[None]


def on_device(*args):
    send_rows, tile_vals = args[5], args[10]
    per_peer, tile = send_rows.shape[3], tile_vals.shape[-1]
    if per_peer % 16 or tile != 128 or args[9].shape[1] > 8 or lax.axis_size("pipe") != CHUNKS:
        return staged_exchange(*args)
    return pipelined(*args)


def solution(mesh):
    placed = (
        P("dom", None),
        P("pipe", None, None),
        P("pipe", None, None),
        P("pipe", None),
        P("pipe", None),
        P("dom", None, None, None),
        P("dom", None, None),
        P("dom", None, None),
        P("dom", None, None),
        P("dom", None),
        P("dom", None, None, None, None),
    )
    return jax.shard_map(
        on_device, mesh=mesh, in_specs=placed, out_specs=P("pipe", "dom", None), check_vma=False
    )
```

```python
import functools

import jax
import jax.numpy as jnp
from jax import lax
from jax.experimental import pallas as pl
from jax.experimental.pallas import tpu as pltpu
from jax.sharding import PartitionSpec as P

MESH = pl.DeviceIdType.MESH
CHUNKS = 4
GROUP = 2
LEAD = 3


def passed_along(block, axis, distance):
    devices = range(lax.axis_size(axis))
    route = [(i - distance, i) for i in devices if i - distance in devices]
    return lax.ppermute(block, axis, route)


def staged_exchange(
    features,
    w_self,
    w_neigh,
    biases,
    gains,
    send_rows,
    send_count,
    tile_dst,
    tile_src,
    tile_count,
    tile_vals,
):
    sections = lax.axis_size("pipe")
    peer_count = lax.axis_size("dom")
    section_no = lax.axis_index("pipe")
    nodes_dev, model_width = features.shape
    stretches = tile_count.shape[1]
    tile_total = tile_src.shape[2]
    tile_size = tile_vals.shape[-1]
    stretch_rows = nodes_dev // stretches
    row_blocks = stretch_rows // tile_size
    per_peer = send_rows.shape[3]
    halo_rows = peer_count * per_peer
    steps_total = stretches + sections - 1
    is_first = section_no == 0
    is_final = section_no == sections - 1
    feature_spans = features.reshape(stretches, stretch_rows, model_width)
    slot_ids = jnp.arange(per_peer, dtype=jnp.int32)
    tile_ids = jnp.arange(tile_total, dtype=jnp.int32)
    block_ids = jnp.arange(row_blocks, dtype=jnp.int32)

    def put_rows(array_in, piece, start, active):
        old_piece = lax.dynamic_slice_in_dim(array_in, start, piece.shape[0], 0)
        return lax.dynamic_update_slice_in_dim(
            array_in, jnp.where(active, piece, old_piece), start, 0
        )

    source_table = jnp.zeros((nodes_dev + stretches * halo_rows, model_width), jnp.bfloat16)
    valid_rows = jnp.concatenate(
        [jnp.ones((nodes_dev,), jnp.float32), jnp.zeros((stretches * halo_rows,), jnp.float32)]
    )
    outputs = jnp.zeros((nodes_dev, model_width), jnp.bfloat16)
    previous = jnp.zeros((stretch_rows, model_width), jnp.bfloat16)
    for step_no in range(steps_total):
        offset = step_no - section_no
        active = (offset >= 0) & (offset < stretches)
        stretch_no = jnp.clip(offset, 0, stretches - 1)
        feed_rows = feature_spans[min(step_no, stretches - 1)]
        if step_no > 0:
            arrived = passed_along(previous, "pipe", 1)
        else:
            arrived = previous
        rows_in = jnp.where(is_first, feed_rows, arrived)
        source_table = put_rows(source_table, rows_in, stretch_no * stretch_rows, active)
        row_picks = lax.dynamic_index_in_dim(send_rows[0], stretch_no, 0, keepdims=False)
        boundary_counts = lax.dynamic_index_in_dim(send_count[0], stretch_no, 0, keepdims=False)
        slot_marks = slot_ids[None, :] < boundary_counts[:, None]
        fetched = jnp.where(slot_marks[:, :, None], rows_in[row_picks], jnp.zeros((), jnp.bfloat16))
        fetched, slot_marks = (fetched, slot_marks.astype(jnp.bfloat16))
        halo_in, marks_in = (
            lax.all_to_all(fetched, "dom", split_axis=0, concat_axis=0, tiled=True),
            lax.all_to_all(slot_marks, "dom", split_axis=0, concat_axis=0, tiled=True),
        )
        aggregate_source_table = source_table
        aggregate_valid_rows = valid_rows
        halo_start = nodes_dev + stretch_no * halo_rows
        aggregate_source_table = put_rows(
            aggregate_source_table, halo_in.reshape(halo_rows, model_width), halo_start, active
        )
        aggregate_valid_rows = put_rows(
            aggregate_valid_rows,
            marks_in.reshape(halo_rows).astype(jnp.float32),
            halo_start,
            active,
        )
        counts = tile_count[0][stretch_no]
        sources = tile_src[0][stretch_no]
        targets = tile_dst[0][stretch_no]
        weights = tile_vals[0][stretch_no]
        live = tile_ids < counts
        picks = ((targets[:, None] == block_ids[None, :]) & live[:, None]).astype(jnp.bfloat16)
        placed = jnp.einsum("tr,tij->ritj", picks, weights, preferred_element_type=jnp.float32)
        dense = placed.astype(jnp.bfloat16).reshape(stretch_rows, tile_total * tile_size)
        gathered = jnp.concatenate(
            [
                lax.dynamic_slice_in_dim(
                    aggregate_source_table, sources[t] * tile_size, tile_size, 0
                )
                for t in range(tile_total)
            ],
            axis=0,
        )
        marks = (
            aggregate_valid_rows.reshape(-1, tile_size)[sources]
            .reshape(tile_total * tile_size)
            .astype(jnp.bfloat16)
        )
        add_summed = jnp.dot(dense, gathered, preferred_element_type=jnp.float32)
        add_degree = jnp.dot(dense, marks, preferred_element_type=jnp.float32)
        source_table = aggregate_source_table
        valid_rows = aggregate_valid_rows
        neighbour = (
            (rows_in.astype(jnp.float32) + add_summed) / (1.0 + add_degree)[:, None]
        ).astype(jnp.bfloat16)
        pre_norm = jnp.dot(rows_in, w_self[0], preferred_element_type=jnp.float32)
        pre_norm = (
            pre_norm
            + jnp.dot(neighbour, w_neigh[0], preferred_element_type=jnp.float32)
            + biases[0]
        )
        normed = (
            gains[0]
            * pre_norm
            * lax.rsqrt(jnp.mean(pre_norm * pre_norm, axis=-1, keepdims=True) + 1e-05)
        )
        previous = jnp.where(is_final, normed, jnp.maximum(normed, 0.0)).astype(jnp.bfloat16)
        outputs = put_rows(outputs, previous, stretch_no * stretch_rows, active)
    return outputs[None]


def layers_kernel(
    stretches,
    feat,
    w_self_hbm,
    w_neigh_hbm,
    bias_hbm,
    gain_hbm,
    listed_hbm,
    counts_hbm,
    dst_hbm,
    src_hbm,
    used_hbm,
    vals_hbm,
    out,
    h,
    staged,
    shared,
    share_out,
    halo_out,
    halo_in,
    marks_out,
    marks_in,
    vals,
    adj,
    picks,
    scales,
    sums,
    z,
    w_self,
    w_neigh,
    bias,
    gain,
    listed,
    counts,
    dst,
    src,
    used,
    h_sem,
    hop_sem,
    halo_send,
    halo_recv,
    share_sem,
    share_send,
    mark_send,
    mark_recv,
    vals_sem,
    w_sem,
    small_sem,
):
    pipes, peers = lax.axis_size("pipe"), lax.axis_size("dom")
    pipe, me = lax.axis_index("pipe"), lax.axis_index("dom")
    _, nodes, part = h.shape
    ch = nodes // stretches
    per_peer = halo_in.shape[3]
    halo = peers * per_peer
    tiles, tile = vals.shape[1:3]
    row_blocks = ch // tile
    pair = GROUP * part

    def rows(c):
        return pl.ds(c * ch, ch)

    def cols(j):
        return pl.ds(j * part, part)

    def arrived(ref, sem):
        pltpu.make_async_copy(ref, ref, sem).wait()

    def dot(a, b):
        return jnp.dot(a, b, preferred_element_type=jnp.float32)

    mine = pl.ds(pl.multiple_of(pipe * part, part), part)
    small = [
        pltpu.make_async_copy(listed_hbm, listed, small_sem.at[0]),
        pltpu.make_async_copy(counts_hbm, counts, small_sem.at[1]),
        pltpu.make_async_copy(dst_hbm, dst, small_sem.at[2]),
        pltpu.make_async_copy(src_hbm, src, small_sem.at[3]),
        pltpu.make_async_copy(used_hbm, used, small_sem.at[4]),
        pltpu.make_async_copy(bias_hbm, bias, small_sem.at[5]),
        pltpu.make_async_copy(gain_hbm, gain, small_sem.at[6]),
    ]
    share_loads = [
        pltpu.make_async_copy(feat.at[rows(c), mine], shared.at[rows(c)], share_sem.at[c])
        for c in range(stretches)
    ]
    tile_loads = [
        pltpu.make_async_copy(vals_hbm.at[0, c], vals.at[c], vals_sem.at[c])
        for c in range(stretches)
    ]
    weights = [
        pltpu.make_async_copy(w_self_hbm.at[0], w_self, w_sem.at[0]),
        pltpu.make_async_copy(w_neigh_hbm.at[0], w_neigh, w_sem.at[1]),
    ]
    for copy in small[:2] + share_loads[:1] + small[2:] + tile_loads[:1]:
        copy.start()

    @pl.when(pipe == 0)
    def _():
        for c in range(stretches):
            for j in range(CHUNKS):
                pltpu.make_async_copy(
                    feat.at[rows(c), cols(j)], h.at[j, rows(c)], h_sem.at[c, j]
                ).start()

    for copy in weights + share_loads[1:] + tile_loads[1:]:
        copy.start()

    barrier = pltpu.get_barrier_semaphore()
    everyone = pipes * peers

    def greet(k, carry):
        other = lax.rem(pipe * peers + me + k, everyone)
        pl.semaphore_signal(
            barrier, inc=1, device_id=(other // peers, lax.rem(other, peers)), device_id_type=MESH
        )
        return carry

    lax.fori_loop(1, everyone, greet, 0)
    small[0].wait()
    small[1].wait()

    slot = lax.broadcasted_iota(jnp.int32, (1, halo), 1)
    row_ids = lax.broadcasted_iota(jnp.int32, (halo, ch), 1)

    def make_pick(c):
        limit = jnp.zeros((1, halo), jnp.int32)
        for p in range(peers):
            limit = jnp.where(slot >= p * per_peer, p * per_peer + counts[0, c, p], limit)
        rows_listed = jnp.concatenate([listed[0, c, p : p + 1, :] for p in range(peers)], axis=1)
        wanted = jnp.where(slot < limit, rows_listed, -1).astype(jnp.float32)
        column = jnp.transpose(jnp.broadcast_to(wanted, (8, halo)))[:, :1].astype(jnp.int32)
        picks[c] = jnp.where(row_ids == column, 1.0, 0.0).astype(jnp.bfloat16)

    def share(c):
        share_loads[c].wait()
        sent = dot(picks[c], shared[rows(c), :])
        share_out[c] = sent.astype(jnp.bfloat16).reshape(peers, per_peer, part)

        def send(k, carry):
            to = lax.rem(me + k, peers)
            pltpu.make_async_remote_copy(
                src_ref=share_out.at[c, to],
                dst_ref=halo_in.at[c, pipe, me],
                send_sem=share_send.at[c],
                recv_sem=halo_recv.at[c, pipe],
                device_id=(0, to),
                device_id_type=MESH,
            ).start()
            return carry

        lax.fori_loop(1, peers, send, 0)

        @pl.when(pipe == 0)
        def _():
            pltpu.make_async_copy(
                share_out.at[c, me], halo_in.at[c, 0, me], halo_recv.at[c, 0]
            ).start()

        @pl.when(pipe > 0)
        def _():
            send(0, 0)

    make_pick(0)
    pl.semaphore_wait(barrier, everyone - 1)
    share(0)

    mark_shape = marks_out.shape[1:]
    mark_row = lax.broadcasted_iota(jnp.int32, mark_shape, 0)
    mark_slot = lax.broadcasted_iota(jnp.int32, mark_shape, 1) - me * per_peer
    for p in range(peers):
        limit = jnp.zeros(mark_shape, jnp.int32)
        for c in range(stretches):
            limit = jnp.where(mark_row == c, counts[0, c, p], limit)
        mark = (mark_slot >= 0) & (mark_slot < limit)
        marks_out[p] = jnp.where(mark, 1.0, 0.0).astype(jnp.bfloat16)

    def send_marks(k, carry):
        to = lax.rem(me + k, peers)
        pltpu.make_async_remote_copy(
            src_ref=marks_out.at[to],
            dst_ref=marks_in.at[me],
            send_sem=mark_send,
            recv_sem=mark_recv,
            device_id=(pipe, to),
            device_id_type=MESH,
        ).start()
        return carry

    lax.fori_loop(1, peers, send_marks, 0)
    pltpu.make_async_copy(marks_out.at[me], marks_in.at[me], mark_recv).start()

    for copy in small[2:5]:
        copy.wait()

    def build(c):
        tile_loads[c].wait()
        codes = [
            jnp.where(t < used[0, c], src[0, c, t] * row_blocks + dst[0, c, t], -1)
            for t in range(tiles)
        ]

        def blocks(first, count):
            def one(i, carry):
                b = first + i
                totals = [jnp.zeros((tile, tile), jnp.float32) for _ in range(row_blocks)]
                for t in range(tiles):
                    weight = vals[c, t].astype(jnp.float32)
                    for r in range(row_blocks):
                        on = jnp.where(codes[t] == b * row_blocks + r, 1.0, 0.0)
                        totals[r] = totals[r] + weight * on
                at = pl.ds(pl.multiple_of(b * tile, tile), tile)
                for r in range(row_blocks):
                    adj[c, r * tile : (r + 1) * tile, at] = totals[r].astype(jnp.bfloat16)
                return carry

            lax.fori_loop(0, count, one, 0)

        blocks(0, (c + 1) * ch // tile)
        blocks(nodes // tile, (c + 1) * halo // tile)

    over_rows = (((1,), (1,)), ((), ()))

    def far(c, d):
        return adj[c, :, nodes + d * halo : nodes + (d + 1) * halo]

    def make_scale(c):
        own = (c + 1) * ch
        valid = marks_in[0]
        for q in range(1, peers):
            valid = valid + marks_in[q]
        ones = jnp.ones((valid.shape[0], own), jnp.bfloat16)
        deg = lax.dot_general(
            adj[c, :, :own], ones, over_rows, preferred_element_type=jnp.float32
        )[:, :1]
        for d in range(c + 1):
            deg = deg + lax.dot_general(
                far(c, d), valid, over_rows, preferred_element_type=jnp.float32
            )[:, d : d + 1]
        scales[c] = jnp.broadcast_to(1.0 / (1.0 + deg), (ch, part))

    def send_chunk(c, j):
        arrived(h.at[j, rows(c)], h_sem.at[c, j])
        sent = dot(picks[c], h[j, rows(c), :])
        halo_out[c, j] = sent.astype(jnp.bfloat16).reshape(peers, per_peer, part)

        def send(k, carry):
            to = lax.rem(me + k, peers)
            pltpu.make_async_remote_copy(
                src_ref=halo_out.at[c, j, to],
                dst_ref=halo_in.at[c, j, me],
                send_sem=halo_send.at[c, j],
                recv_sem=halo_recv.at[c, j],
                device_id=(pipe, to),
                device_id_type=MESH,
            ).start()
            return carry

        lax.fori_loop(1, peers, send, 0)
        pltpu.make_async_copy(
            halo_out.at[c, j, me], halo_in.at[c, j, me], halo_recv.at[c, j]
        ).start()

    def near_sums(c, js):
        own = (c + 1) * ch
        span = pl.ds(js[0] * part, len(js) * part)
        held = jnp.concatenate([h[j, rows(c), :] for j in js], axis=1)
        before = bias[...] if js[0] == 0 else z[...]
        z[...] = before + dot(held, w_self[span, :])
        added = held.astype(jnp.float32) + dot(
            adj[c, :, :own], jnp.concatenate([h[j, :own, :] for j in js], axis=1)
        )
        for d in range(c):
            added = added + dot(
                far(c, d), jnp.concatenate([halo_in[d, j].reshape(halo, part) for j in js], axis=1)
            )
        sums[:, span] = added

    def far_sums(c, js):
        for j in js:
            arrived(halo_in.at[c, j], halo_recv.at[c, j])
        fetched = jnp.concatenate([halo_in[c, j].reshape(halo, part) for j in js], axis=1)
        span = pl.ds(js[0] * part, len(js) * part)
        scale = jnp.concatenate([scales[c]] * len(js), axis=1)
        agg = (sums[:, span] + dot(far(c, c), fetched)) * scale
        z[...] += dot(agg.astype(jnp.bfloat16), w_neigh[span, :])

    floor = jnp.where(pipe == pipes - 1, -jnp.inf, 0.0).astype(jnp.float32)

    def finish(c):
        value = z[...]
        u = gain[...] * value * lax.rsqrt(jnp.mean(value * value, axis=-1, keepdims=True) + 1e-05)
        result = jnp.maximum(u, floor).astype(jnp.bfloat16)

        def hop(j):
            staged[j, rows(c), :] = result[:, j * part : (j + 1) * part]
            pltpu.make_async_remote_copy(
                src_ref=staged.at[j, rows(c)],
                dst_ref=h.at[j, rows(c)],
                send_sem=hop_sem.at[c, j],
                recv_sem=h_sem.at[c, j],
                device_id=(pipe + 1, me),
                device_id_type=MESH,
            ).start()

        @pl.when(pipe < pipes - 1)
        def _():
            for j in range(CHUNKS):
                hop(j)

        out[rows(c), :] = result

    def wait_weights():
        for copy in weights + small[5:]:
            copy.wait()

    build(0)

    @pl.when(pipe == 0)
    def _():
        for c in range(stretches):
            for j in range(CHUNKS):
                arrived(h.at[j, rows(c)], h_sem.at[c, j])
            if c == 0:
                wait_weights()
            near_sums(c, (0, 1))
            near_sums(c, (2, 3))
            if c == 0:
                make_pick(1)
                share(1)
                arrived(marks_in, mark_recv)
            make_scale(c)
            for j in range(CHUNKS):
                far_sums(c, (j,))
            finish(c)
            if c + 2 < stretches:
                make_pick(c + 2)
                share(c + 2)
            if c + 1 < stretches:
                build(c + 1)

    @pl.when(pipe > 0)
    def _():
        build(1)
        build(2)
        make_pick(1)
        share(1)
        build(3)
        make_pick(2)
        share(2)
        arrived(marks_in, mark_recv)
        for c in range(stretches):
            make_scale(c)
        wait_weights()
        make_pick(3)
        share(3)
        for j in range(CHUNKS):
            send_chunk(0, j)
        for c in range(stretches):
            near_sums(c, (0, 1))
            near_sums(c, (2, 3))
            for j in range(CHUNKS):
                if c + 1 < stretches and CHUNKS - j <= LEAD:
                    send_chunk(c + 1, j + LEAD - CHUNKS)
                far_sums(c, (j,))
            finish(c)
            if c + 1 < stretches:
                for j in range(LEAD, CHUNKS):
                    send_chunk(c + 1, j)

    others = pl.ds(0, peers - 1)
    arrived(marks_out.at[others], mark_send)

    @pl.when(pipe == 0)
    def _():
        for c in range(stretches):
            arrived(share_out.at[c, others], share_send.at[c])

    @pl.when(pipe > 0)
    def _():
        for c in range(stretches):
            arrived(share_out.at[c], share_send.at[c])
            for j in range(CHUNKS):
                arrived(halo_out.at[c, j, others], halo_send.at[c, j])

    @pl.when(pipe < pipes - 1)
    def _():
        for c in range(stretches):
            for j in range(CHUNKS):
                arrived(staged.at[j, rows(c)], hop_sem.at[c, j])


def pipelined(
    features,
    w_self,
    w_neigh,
    biases,
    gains,
    send_rows,
    send_count,
    tile_dst,
    tile_src,
    tile_count,
    tile_vals,
):
    peers = lax.axis_size("dom")
    nodes, width = features.shape
    stretches = tile_count.shape[1]
    per_peer = send_rows.shape[3]
    ch = nodes // stretches
    halo = peers * per_peer
    part = width // CHUNKS
    sources = nodes + stretches * halo
    tiles = tile_vals.shape[1:]
    anywhere = pl.BlockSpec(memory_space=pltpu.HBM)
    halo_shape = (stretches, CHUNKS, peers, per_peer, part)
    out = pl.pallas_call(
        functools.partial(layers_kernel, stretches),
        out_shape=pltpu.VMEM((nodes, width), jnp.bfloat16),
        in_specs=[anywhere] * 11,
        out_specs=pl.BlockSpec(memory_space=pltpu.VMEM),
        scratch_shapes=[
            pltpu.VMEM((CHUNKS, nodes, part), jnp.bfloat16),
            pltpu.VMEM((CHUNKS, nodes, part), jnp.bfloat16),
            pltpu.VMEM((nodes, part), jnp.bfloat16),
            pltpu.VMEM((stretches, peers, per_peer, part), jnp.bfloat16),
            pltpu.VMEM(halo_shape, jnp.bfloat16),
            pltpu.VMEM(halo_shape, jnp.bfloat16),
            pltpu.VMEM((peers, 8, halo), jnp.bfloat16),
            pltpu.VMEM((peers, 8, halo), jnp.bfloat16),
            pltpu.VMEM(tiles, jnp.bfloat16),
            pltpu.VMEM((stretches, ch, sources), jnp.bfloat16),
            pltpu.VMEM((stretches, halo, ch), jnp.bfloat16),
            pltpu.VMEM((stretches, ch, part), jnp.float32),
            pltpu.VMEM((ch, width), jnp.float32),
            pltpu.VMEM((ch, width), jnp.float32),
            pltpu.VMEM((width, width), jnp.bfloat16),
            pltpu.VMEM((width, width), jnp.bfloat16),
            pltpu.VMEM(biases.shape, jnp.float32),
            pltpu.VMEM(gains.shape, jnp.float32),
            pltpu.VMEM(send_rows.shape, jnp.int32),
            pltpu.SMEM(send_count.shape, jnp.int32),
            pltpu.SMEM(tile_dst.shape, jnp.int32),
            pltpu.SMEM(tile_src.shape, jnp.int32),
            pltpu.SMEM(tile_count.shape, jnp.int32),
            pltpu.SemaphoreType.DMA((stretches, CHUNKS)),
            pltpu.SemaphoreType.DMA((stretches, CHUNKS)),
            pltpu.SemaphoreType.DMA((stretches, CHUNKS)),
            pltpu.SemaphoreType.DMA((stretches, CHUNKS)),
            pltpu.SemaphoreType.DMA((stretches,)),
            pltpu.SemaphoreType.DMA((stretches,)),
            pltpu.SemaphoreType.DMA,
            pltpu.SemaphoreType.DMA,
            pltpu.SemaphoreType.DMA((stretches,)),
            pltpu.SemaphoreType.DMA((2,)),
            pltpu.SemaphoreType.DMA((7,)),
        ],
        compiler_params=pltpu.CompilerParams(
            collective_id=0, has_side_effects=True, vmem_limit_bytes=40 * 2**20
        ),
        name="layers",
    )(
        *(
            pltpu.with_memory_space_constraint(array, pltpu.HBM)
            for array in (
                features,
                w_self,
                w_neigh,
                biases,
                gains,
                send_rows,
                send_count,
                tile_dst,
                tile_src,
                tile_count,
                tile_vals,
            )
        )
    )
    return out[None]


def on_device(*args):
    send_rows, tile_vals = args[5], args[10]
    per_peer, tile = send_rows.shape[3], tile_vals.shape[-1]
    if per_peer % 16 or tile != 128 or args[9].shape[1] > 8 or lax.axis_size("pipe") != CHUNKS:
        return staged_exchange(*args)
    return pipelined(*args)


def solution(mesh):
    placed = (
        P("dom", None),
        P("pipe", None, None),
        P("pipe", None, None),
        P("pipe", None),
        P("pipe", None),
        P("dom", None, None, None),
        P("dom", None, None),
        P("dom", None, None),
        P("dom", None, None),
        P("dom", None),
        P("dom", None, None, None, None),
    )
    return jax.shard_map(
        on_device, mesh=mesh, in_specs=placed, out_specs=P("pipe", "dom", None), check_vma=False
    )
```

```python
import functools

import jax
import jax.numpy as jnp
from jax import lax
from jax.experimental import pallas as pl
from jax.experimental.pallas import tpu as pltpu
from jax.sharding import PartitionSpec as P

MESH = pl.DeviceIdType.MESH
CHUNKS = 4
GROUP = 2
LEAD = 3


def passed_along(block, axis, distance):
    devices = range(lax.axis_size(axis))
    route = [(i - distance, i) for i in devices if i - distance in devices]
    return lax.ppermute(block, axis, route)


def staged_exchange(
    features,
    w_self,
    w_neigh,
    biases,
    gains,
    send_rows,
    send_count,
    tile_dst,
    tile_src,
    tile_count,
    tile_vals,
):
    sections = lax.axis_size("pipe")
    peer_count = lax.axis_size("dom")
    section_no = lax.axis_index("pipe")
    nodes_dev, model_width = features.shape
    stretches = tile_count.shape[1]
    tile_total = tile_src.shape[2]
    tile_size = tile_vals.shape[-1]
    stretch_rows = nodes_dev // stretches
    row_blocks = stretch_rows // tile_size
    per_peer = send_rows.shape[3]
    halo_rows = peer_count * per_peer
    steps_total = stretches + sections - 1
    is_first = section_no == 0
    is_final = section_no == sections - 1
    feature_spans = features.reshape(stretches, stretch_rows, model_width)
    slot_ids = jnp.arange(per_peer, dtype=jnp.int32)
    tile_ids = jnp.arange(tile_total, dtype=jnp.int32)
    block_ids = jnp.arange(row_blocks, dtype=jnp.int32)

    def put_rows(array_in, piece, start, active):
        old_piece = lax.dynamic_slice_in_dim(array_in, start, piece.shape[0], 0)
        return lax.dynamic_update_slice_in_dim(
            array_in, jnp.where(active, piece, old_piece), start, 0
        )

    source_table = jnp.zeros((nodes_dev + stretches * halo_rows, model_width), jnp.bfloat16)
    valid_rows = jnp.concatenate(
        [jnp.ones((nodes_dev,), jnp.float32), jnp.zeros((stretches * halo_rows,), jnp.float32)]
    )
    outputs = jnp.zeros((nodes_dev, model_width), jnp.bfloat16)
    previous = jnp.zeros((stretch_rows, model_width), jnp.bfloat16)
    for step_no in range(steps_total):
        offset = step_no - section_no
        active = (offset >= 0) & (offset < stretches)
        stretch_no = jnp.clip(offset, 0, stretches - 1)
        feed_rows = feature_spans[min(step_no, stretches - 1)]
        if step_no > 0:
            arrived = passed_along(previous, "pipe", 1)
        else:
            arrived = previous
        rows_in = jnp.where(is_first, feed_rows, arrived)
        source_table = put_rows(source_table, rows_in, stretch_no * stretch_rows, active)
        row_picks = lax.dynamic_index_in_dim(send_rows[0], stretch_no, 0, keepdims=False)
        boundary_counts = lax.dynamic_index_in_dim(send_count[0], stretch_no, 0, keepdims=False)
        slot_marks = slot_ids[None, :] < boundary_counts[:, None]
        fetched = jnp.where(slot_marks[:, :, None], rows_in[row_picks], jnp.zeros((), jnp.bfloat16))
        fetched, slot_marks = (fetched, slot_marks.astype(jnp.bfloat16))
        halo_in, marks_in = (
            lax.all_to_all(fetched, "dom", split_axis=0, concat_axis=0, tiled=True),
            lax.all_to_all(slot_marks, "dom", split_axis=0, concat_axis=0, tiled=True),
        )
        aggregate_source_table = source_table
        aggregate_valid_rows = valid_rows
        halo_start = nodes_dev + stretch_no * halo_rows
        aggregate_source_table = put_rows(
            aggregate_source_table, halo_in.reshape(halo_rows, model_width), halo_start, active
        )
        aggregate_valid_rows = put_rows(
            aggregate_valid_rows,
            marks_in.reshape(halo_rows).astype(jnp.float32),
            halo_start,
            active,
        )
        counts = tile_count[0][stretch_no]
        sources = tile_src[0][stretch_no]
        targets = tile_dst[0][stretch_no]
        weights = tile_vals[0][stretch_no]
        live = tile_ids < counts
        picks = ((targets[:, None] == block_ids[None, :]) & live[:, None]).astype(jnp.bfloat16)
        placed = jnp.einsum("tr,tij->ritj", picks, weights, preferred_element_type=jnp.float32)
        dense = placed.astype(jnp.bfloat16).reshape(stretch_rows, tile_total * tile_size)
        gathered = jnp.concatenate(
            [
                lax.dynamic_slice_in_dim(
                    aggregate_source_table, sources[t] * tile_size, tile_size, 0
                )
                for t in range(tile_total)
            ],
            axis=0,
        )
        marks = (
            aggregate_valid_rows.reshape(-1, tile_size)[sources]
            .reshape(tile_total * tile_size)
            .astype(jnp.bfloat16)
        )
        add_summed = jnp.dot(dense, gathered, preferred_element_type=jnp.float32)
        add_degree = jnp.dot(dense, marks, preferred_element_type=jnp.float32)
        source_table = aggregate_source_table
        valid_rows = aggregate_valid_rows
        neighbour = (
            (rows_in.astype(jnp.float32) + add_summed) / (1.0 + add_degree)[:, None]
        ).astype(jnp.bfloat16)
        pre_norm = jnp.dot(rows_in, w_self[0], preferred_element_type=jnp.float32)
        pre_norm = (
            pre_norm
            + jnp.dot(neighbour, w_neigh[0], preferred_element_type=jnp.float32)
            + biases[0]
        )
        normed = (
            gains[0]
            * pre_norm
            * lax.rsqrt(jnp.mean(pre_norm * pre_norm, axis=-1, keepdims=True) + 1e-05)
        )
        previous = jnp.where(is_final, normed, jnp.maximum(normed, 0.0)).astype(jnp.bfloat16)
        outputs = put_rows(outputs, previous, stretch_no * stretch_rows, active)
    return outputs[None]


def layers_kernel(
    stretches,
    feat,
    w_self_hbm,
    w_neigh_hbm,
    bias_hbm,
    gain_hbm,
    listed_hbm,
    counts_hbm,
    dst_hbm,
    src_hbm,
    used_hbm,
    vals_hbm,
    out,
    h,
    staged,
    shared,
    share_out,
    halo_out,
    halo_in,
    marks_out,
    marks_in,
    vals,
    adj,
    picks,
    scales,
    sums,
    z,
    w_self,
    w_neigh,
    bias,
    gain,
    listed,
    counts,
    dst,
    src,
    used,
    h_sem,
    hop_sem,
    halo_send,
    halo_recv,
    share_sem,
    share_send,
    mark_send,
    mark_recv,
    vals_sem,
    w_sem,
    small_sem,
):
    pipes, peers = lax.axis_size("pipe"), lax.axis_size("dom")
    pipe, me = lax.axis_index("pipe"), lax.axis_index("dom")
    _, nodes, part = h.shape
    ch = nodes // stretches
    per_peer = halo_in.shape[3]
    halo = peers * per_peer
    tiles, tile = vals.shape[1:3]
    row_blocks = ch // tile
    pair = GROUP * part

    def rows(c):
        return pl.ds(c * ch, ch)

    def cols(j):
        return pl.ds(j * part, part)

    def arrived(ref, sem):
        pltpu.make_async_copy(ref, ref, sem).wait()

    def dot(a, b):
        return jnp.dot(a, b, preferred_element_type=jnp.float32)

    barrier = pltpu.get_barrier_semaphore()
    everyone = pipes * peers

    def greet(k, carry):
        other = lax.rem(pipe * peers + me + k, everyone)
        pl.semaphore_signal(
            barrier, inc=1, device_id=(other // peers, lax.rem(other, peers)), device_id_type=MESH
        )
        return carry

    def greet_peers():
        def one(k, carry):
            pl.semaphore_signal(
                barrier, inc=1, device_id=(pipe, lax.rem(me + k, peers)), device_id_type=MESH
            )
            return carry

        lax.fori_loop(1, peers, one, 0)
        pl.semaphore_signal(barrier, inc=1, device_id=(pipe - 1, me), device_id_type=MESH)

    @pl.when(pipe == 0)
    def _():
        lax.fori_loop(1, everyone, greet, 0)

    @pl.when(pipe > 0)
    def _():
        greet_peers()

    mine = pl.ds(pl.multiple_of(pipe * part, part), part)
    small = [
        pltpu.make_async_copy(listed_hbm, listed, small_sem.at[0]),
        pltpu.make_async_copy(counts_hbm, counts, small_sem.at[1]),
        pltpu.make_async_copy(dst_hbm, dst, small_sem.at[2]),
        pltpu.make_async_copy(src_hbm, src, small_sem.at[3]),
        pltpu.make_async_copy(used_hbm, used, small_sem.at[4]),
        pltpu.make_async_copy(bias_hbm, bias, small_sem.at[5]),
        pltpu.make_async_copy(gain_hbm, gain, small_sem.at[6]),
    ]
    share_loads = [
        pltpu.make_async_copy(feat.at[rows(c), mine], shared.at[rows(c)], share_sem.at[c])
        for c in range(stretches)
    ]
    tile_loads = [
        pltpu.make_async_copy(vals_hbm.at[0, c], vals.at[c], vals_sem.at[c])
        for c in range(stretches)
    ]
    weights = [
        pltpu.make_async_copy(w_self_hbm.at[0], w_self, w_sem.at[0]),
        pltpu.make_async_copy(w_neigh_hbm.at[0], w_neigh, w_sem.at[1]),
    ]
    for copy in small[:2] + share_loads[:1] + small[2:] + tile_loads[:1]:
        copy.start()

    @pl.when(pipe == 0)
    def _():
        for c in range(stretches):
            for j in range(CHUNKS):
                pltpu.make_async_copy(
                    feat.at[rows(c), cols(j)], h.at[j, rows(c)], h_sem.at[c, j]
                ).start()

    for copy in weights + share_loads[1:] + tile_loads[1:]:
        copy.start()

    small[0].wait()
    small[1].wait()

    slot = lax.broadcasted_iota(jnp.int32, (1, halo), 1)
    row_ids = lax.broadcasted_iota(jnp.int32, (halo, ch), 1)

    def make_pick(c):
        limit = jnp.zeros((1, halo), jnp.int32)
        for p in range(peers):
            limit = jnp.where(slot >= p * per_peer, p * per_peer + counts[0, c, p], limit)
        rows_listed = jnp.concatenate([listed[0, c, p : p + 1, :] for p in range(peers)], axis=1)
        wanted = jnp.where(slot < limit, rows_listed, -1).astype(jnp.float32)
        column = jnp.transpose(jnp.broadcast_to(wanted, (8, halo)))[:, :1].astype(jnp.int32)
        picks[c] = jnp.where(row_ids == column, 1.0, 0.0).astype(jnp.bfloat16)

    def share(c):
        share_loads[c].wait()
        sent = dot(picks[c], shared[rows(c), :])
        share_out[c] = sent.astype(jnp.bfloat16).reshape(peers, per_peer, part)

        def send(k, carry):
            to = lax.rem(me + k, peers)
            pltpu.make_async_remote_copy(
                src_ref=share_out.at[c, to],
                dst_ref=halo_in.at[c, pipe, me],
                send_sem=share_send.at[c],
                recv_sem=halo_recv.at[c, pipe],
                device_id=(0, to),
                device_id_type=MESH,
            ).start()
            return carry

        def fan_out():
            lax.fori_loop(1, peers, send, 0)

            @pl.when(pipe == 0)
            def _():
                pltpu.make_async_copy(
                    share_out.at[c, me], halo_in.at[c, 0, me], halo_recv.at[c, 0]
                ).start()

            @pl.when(pipe > 0)
            def _():
                send(0, 0)

        if c == 0:
            fan_out()
        else:
            pl.when(pipe != 1)(fan_out)

            @pl.when(pipe == 0)
            def _():
                send_picked(c, 1)

    make_pick(0)

    later = jnp.where(pipe < pipes - 1, 2 * peers, 2 * peers - 1)
    pl.semaphore_wait(barrier, jnp.where(pipe == 0, peers, later))
    share(0)

    mark_shape = marks_out.shape[1:]
    mark_row = lax.broadcasted_iota(jnp.int32, mark_shape, 0)
    mark_slot = lax.broadcasted_iota(jnp.int32, mark_shape, 1) - me * per_peer
    for p in range(peers):
        limit = jnp.zeros(mark_shape, jnp.int32)
        for c in range(stretches):
            limit = jnp.where(mark_row == c, counts[0, c, p], limit)
        mark = (mark_slot >= 0) & (mark_slot < limit)
        marks_out[p] = jnp.where(mark, 1.0, 0.0).astype(jnp.bfloat16)

    def send_marks(k, carry):
        to = lax.rem(me + k, peers)
        pltpu.make_async_remote_copy(
            src_ref=marks_out.at[to],
            dst_ref=marks_in.at[me],
            send_sem=mark_send,
            recv_sem=mark_recv,
            device_id=(pipe, to),
            device_id_type=MESH,
        ).start()
        return carry

    lax.fori_loop(1, peers, send_marks, 0)
    pltpu.make_async_copy(marks_out.at[me], marks_in.at[me], mark_recv).start()

    for copy in small[2:5]:
        copy.wait()

    def build(c):
        tile_loads[c].wait()
        codes = [
            jnp.where(t < used[0, c], src[0, c, t] * row_blocks + dst[0, c, t], -1)
            for t in range(tiles)
        ]

        def blocks(first, count):
            def one(i, carry):
                b = first + i
                totals = [jnp.zeros((tile, tile), jnp.float32) for _ in range(row_blocks)]
                for t in range(tiles):
                    weight = vals[c, t].astype(jnp.float32)
                    for r in range(row_blocks):
                        on = jnp.where(codes[t] == b * row_blocks + r, 1.0, 0.0)
                        totals[r] = totals[r] + weight * on
                at = pl.ds(pl.multiple_of(b * tile, tile), tile)
                for r in range(row_blocks):
                    adj[c, r * tile : (r + 1) * tile, at] = totals[r].astype(jnp.bfloat16)
                return carry

            lax.fori_loop(0, count, one, 0)

        blocks(0, (c + 1) * ch // tile)
        blocks(nodes // tile, (c + 1) * halo // tile)

    over_rows = (((1,), (1,)), ((), ()))

    def far(c, d):
        return adj[c, :, nodes + d * halo : nodes + (d + 1) * halo]

    def make_scale(c):
        own = (c + 1) * ch
        valid = marks_in[0]
        for q in range(1, peers):
            valid = valid + marks_in[q]
        ones = jnp.ones((valid.shape[0], own), jnp.bfloat16)
        deg = lax.dot_general(
            adj[c, :, :own], ones, over_rows, preferred_element_type=jnp.float32
        )[:, :1]
        for d in range(c + 1):
            deg = deg + lax.dot_general(
                far(c, d), valid, over_rows, preferred_element_type=jnp.float32
            )[:, d : d + 1]
        scales[c] = jnp.broadcast_to(1.0 / (1.0 + deg), (ch, part))

    def send_chunk(c, j):
        arrived(h.at[j, rows(c)], h_sem.at[c, j])
        send_picked(c, j)

    def send_picked(c, j):
        sent = dot(picks[c], h[j, rows(c), :])
        halo_out[c, j] = sent.astype(jnp.bfloat16).reshape(peers, per_peer, part)

        def send(k, carry):
            down = peers - k - jnp.where(peers - k <= me, 1, 0)
            up = k - 1 + jnp.where(k - 1 >= me, 1, 0)
            to = jnp.where(me < peers // 2, down, up)
            pltpu.make_async_remote_copy(
                src_ref=halo_out.at[c, j, to],
                dst_ref=halo_in.at[c, j, me],
                send_sem=halo_send.at[c, j],
                recv_sem=halo_recv.at[c, j],
                device_id=(pipe, to),
                device_id_type=MESH,
            ).start()
            return carry

        lax.fori_loop(1, peers, send, 0)
        pltpu.make_async_copy(
            halo_out.at[c, j, me], halo_in.at[c, j, me], halo_recv.at[c, j]
        ).start()

    def near_sums(c, js):
        own = (c + 1) * ch
        span = pl.ds(js[0] * part, len(js) * part)
        held = jnp.concatenate([h[j, rows(c), :] for j in js], axis=1)
        before = bias[...] if js[0] == 0 else z[...]
        z[...] = before + dot(held, w_self[span, :])
        added = held.astype(jnp.float32) + dot(
            adj[c, :, :own], jnp.concatenate([h[j, :own, :] for j in js], axis=1)
        )
        for d in range(c):
            added = added + dot(
                far(c, d), jnp.concatenate([halo_in[d, j].reshape(halo, part) for j in js], axis=1)
            )
        sums[:, span] = added

    def far_sums(c, js):
        for j in js:
            arrived(halo_in.at[c, j], halo_recv.at[c, j])
        fetched = jnp.concatenate([halo_in[c, j].reshape(halo, part) for j in js], axis=1)
        span = pl.ds(js[0] * part, len(js) * part)
        scale = jnp.concatenate([scales[c]] * len(js), axis=1)
        agg = (sums[:, span] + dot(far(c, c), fetched)) * scale
        z[...] += dot(agg.astype(jnp.bfloat16), w_neigh[span, :])

    floor = jnp.where(pipe == pipes - 1, -jnp.inf, 0.0).astype(jnp.float32)

    def finish(c):
        value = z[...]
        u = gain[...] * value * lax.rsqrt(jnp.mean(value * value, axis=-1, keepdims=True) + 1e-05)
        result = jnp.maximum(u, floor).astype(jnp.bfloat16)

        def hop(j):
            staged[j, rows(c), :] = result[:, j * part : (j + 1) * part]
            pltpu.make_async_remote_copy(
                src_ref=staged.at[j, rows(c)],
                dst_ref=h.at[j, rows(c)],
                send_sem=hop_sem.at[c, j],
                recv_sem=h_sem.at[c, j],
                device_id=(pipe + 1, me),
                device_id_type=MESH,
            ).start()

        @pl.when(pipe < pipes - 1)
        def _():
            for j in range(CHUNKS):
                hop(j)

        out[rows(c), :] = result

    def wait_weights():
        for copy in weights + small[5:]:
            copy.wait()

    build(0)

    @pl.when(pipe == 0)
    def _():
        for c in range(stretches):
            if c == 0:
                for d in range(stretches):
                    for j in range(CHUNKS):
                        arrived(h.at[j, rows(d)], h_sem.at[d, j])
                wait_weights()
            near_sums(c, (0, 1))
            near_sums(c, (2, 3))
            if c == 0:
                make_pick(1)
                share(1)
                arrived(marks_in, mark_recv)
            make_scale(c)
            for j in range(CHUNKS):
                far_sums(c, (j,))
            finish(c)
            if c + 2 < stretches:
                make_pick(c + 2)
                share(c + 2)
            if c + 1 < stretches:
                build(c + 1)

    @pl.when(pipe > 0)
    def _():
        build(1)
        build(2)
        make_pick(1)
        share(1)
        build(3)
        make_pick(2)
        share(2)
        arrived(marks_in, mark_recv)
        for c in range(stretches):
            make_scale(c)
        wait_weights()
        make_pick(3)
        share(3)
        for j in range(CHUNKS):
            send_chunk(0, j)
        for c in range(stretches):
            near_sums(c, (0, 1))
            near_sums(c, (2, 3))
            for j in range(CHUNKS):
                if c + 1 < stretches and CHUNKS - j <= LEAD:
                    send_chunk(c + 1, j + LEAD - CHUNKS)
                far_sums(c, (j,))
            finish(c)
            if c + 1 < stretches:
                for j in range(LEAD, CHUNKS):
                    send_chunk(c + 1, j)

    others = pl.ds(0, peers - 1)
    arrived(marks_out.at[others], mark_send)

    @pl.when(pipe == 0)
    def _():
        for c in range(stretches):
            arrived(share_out.at[c, others], share_send.at[c])
            if c > 0:
                arrived(halo_out.at[c, 1, others], halo_send.at[c, 1])

    @pl.when(pipe > 0)
    def _():
        for c in range(stretches):
            if c == 0:
                arrived(share_out.at[c], share_send.at[c])
            else:

                @pl.when(pipe > 1)
                def _():
                    arrived(share_out.at[c], share_send.at[c])

            for j in range(CHUNKS):
                arrived(halo_out.at[c, j, others], halo_send.at[c, j])

    @pl.when(pipe < pipes - 1)
    def _():
        for c in range(stretches):
            for j in range(CHUNKS):
                arrived(staged.at[j, rows(c)], hop_sem.at[c, j])


def pipelined(
    features,
    w_self,
    w_neigh,
    biases,
    gains,
    send_rows,
    send_count,
    tile_dst,
    tile_src,
    tile_count,
    tile_vals,
):
    peers = lax.axis_size("dom")
    nodes, width = features.shape
    stretches = tile_count.shape[1]
    per_peer = send_rows.shape[3]
    ch = nodes // stretches
    halo = peers * per_peer
    part = width // CHUNKS
    sources = nodes + stretches * halo
    tiles = tile_vals.shape[1:]
    anywhere = pl.BlockSpec(memory_space=pltpu.HBM)
    halo_shape = (stretches, CHUNKS, peers, per_peer, part)
    out = pl.pallas_call(
        functools.partial(layers_kernel, stretches),
        out_shape=pltpu.VMEM((nodes, width), jnp.bfloat16),
        in_specs=[anywhere] * 11,
        out_specs=pl.BlockSpec(memory_space=pltpu.VMEM),
        scratch_shapes=[
            pltpu.VMEM((CHUNKS, nodes, part), jnp.bfloat16),
            pltpu.VMEM((CHUNKS, nodes, part), jnp.bfloat16),
            pltpu.VMEM((nodes, part), jnp.bfloat16),
            pltpu.VMEM((stretches, peers, per_peer, part), jnp.bfloat16),
            pltpu.VMEM(halo_shape, jnp.bfloat16),
            pltpu.VMEM(halo_shape, jnp.bfloat16),
            pltpu.VMEM((peers, 8, halo), jnp.bfloat16),
            pltpu.VMEM((peers, 8, halo), jnp.bfloat16),
            pltpu.VMEM(tiles, jnp.bfloat16),
            pltpu.VMEM((stretches, ch, sources), jnp.bfloat16),
            pltpu.VMEM((stretches, halo, ch), jnp.bfloat16),
            pltpu.VMEM((stretches, ch, part), jnp.float32),
            pltpu.VMEM((ch, width), jnp.float32),
            pltpu.VMEM((ch, width), jnp.float32),
            pltpu.VMEM((width, width), jnp.bfloat16),
            pltpu.VMEM((width, width), jnp.bfloat16),
            pltpu.VMEM(biases.shape, jnp.float32),
            pltpu.VMEM(gains.shape, jnp.float32),
            pltpu.VMEM(send_rows.shape, jnp.int32),
            pltpu.SMEM(send_count.shape, jnp.int32),
            pltpu.SMEM(tile_dst.shape, jnp.int32),
            pltpu.SMEM(tile_src.shape, jnp.int32),
            pltpu.SMEM(tile_count.shape, jnp.int32),
            pltpu.SemaphoreType.DMA((stretches, CHUNKS)),
            pltpu.SemaphoreType.DMA((stretches, CHUNKS)),
            pltpu.SemaphoreType.DMA((stretches, CHUNKS)),
            pltpu.SemaphoreType.DMA((stretches, CHUNKS)),
            pltpu.SemaphoreType.DMA((stretches,)),
            pltpu.SemaphoreType.DMA((stretches,)),
            pltpu.SemaphoreType.DMA,
            pltpu.SemaphoreType.DMA,
            pltpu.SemaphoreType.DMA((stretches,)),
            pltpu.SemaphoreType.DMA((2,)),
            pltpu.SemaphoreType.DMA((7,)),
        ],
        compiler_params=pltpu.CompilerParams(
            collective_id=0, has_side_effects=True, vmem_limit_bytes=40 * 2**20
        ),
        name="layers",
    )(
        *(
            pltpu.with_memory_space_constraint(array, pltpu.HBM)
            for array in (
                features,
                w_self,
                w_neigh,
                biases,
                gains,
                send_rows,
                send_count,
                tile_dst,
                tile_src,
                tile_count,
                tile_vals,
            )
        )
    )
    return out[None]


def on_device(*args):
    send_rows, tile_vals = args[5], args[10]
    per_peer, tile = send_rows.shape[3], tile_vals.shape[-1]
    if per_peer % 16 or tile != 128 or args[9].shape[1] > 8 or lax.axis_size("pipe") != CHUNKS:
        return staged_exchange(*args)
    return pipelined(*args)


def solution(mesh):
    placed = (
        P("dom", None),
        P("pipe", None, None),
        P("pipe", None, None),
        P("pipe", None),
        P("pipe", None),
        P("dom", None, None, None),
        P("dom", None, None),
        P("dom", None, None),
        P("dom", None, None),
        P("dom", None),
        P("dom", None, None, None, None),
    )
    return jax.shard_map(
        on_device, mesh=mesh, in_specs=placed, out_specs=P("pipe", "dom", None), check_vma=False
    )
```

```python
import functools

import jax
import jax.numpy as jnp
from jax import lax
from jax.experimental import pallas as pl
from jax.experimental.pallas import tpu as pltpu
from jax.sharding import PartitionSpec as P

MESH = pl.DeviceIdType.MESH
CHUNKS = 4
GROUP = 2
LEAD = 3


def passed_along(block, axis, distance):
    devices = range(lax.axis_size(axis))
    route = [(i - distance, i) for i in devices if i - distance in devices]
    return lax.ppermute(block, axis, route)


def staged_exchange(
    features,
    w_self,
    w_neigh,
    biases,
    gains,
    send_rows,
    send_count,
    tile_dst,
    tile_src,
    tile_count,
    tile_vals,
):
    sections = lax.axis_size("pipe")
    peer_count = lax.axis_size("dom")
    section_no = lax.axis_index("pipe")
    nodes_dev, model_width = features.shape
    stretches = tile_count.shape[1]
    tile_total = tile_src.shape[2]
    tile_size = tile_vals.shape[-1]
    stretch_rows = nodes_dev // stretches
    row_blocks = stretch_rows // tile_size
    per_peer = send_rows.shape[3]
    halo_rows = peer_count * per_peer
    steps_total = stretches + sections - 1
    is_first = section_no == 0
    is_final = section_no == sections - 1
    feature_spans = features.reshape(stretches, stretch_rows, model_width)
    slot_ids = jnp.arange(per_peer, dtype=jnp.int32)
    tile_ids = jnp.arange(tile_total, dtype=jnp.int32)
    block_ids = jnp.arange(row_blocks, dtype=jnp.int32)

    def put_rows(array_in, piece, start, active):
        old_piece = lax.dynamic_slice_in_dim(array_in, start, piece.shape[0], 0)
        return lax.dynamic_update_slice_in_dim(
            array_in, jnp.where(active, piece, old_piece), start, 0
        )

    source_table = jnp.zeros((nodes_dev + stretches * halo_rows, model_width), jnp.bfloat16)
    valid_rows = jnp.concatenate(
        [jnp.ones((nodes_dev,), jnp.float32), jnp.zeros((stretches * halo_rows,), jnp.float32)]
    )
    outputs = jnp.zeros((nodes_dev, model_width), jnp.bfloat16)
    previous = jnp.zeros((stretch_rows, model_width), jnp.bfloat16)
    for step_no in range(steps_total):
        offset = step_no - section_no
        active = (offset >= 0) & (offset < stretches)
        stretch_no = jnp.clip(offset, 0, stretches - 1)
        feed_rows = feature_spans[min(step_no, stretches - 1)]
        if step_no > 0:
            arrived = passed_along(previous, "pipe", 1)
        else:
            arrived = previous
        rows_in = jnp.where(is_first, feed_rows, arrived)
        source_table = put_rows(source_table, rows_in, stretch_no * stretch_rows, active)
        row_picks = lax.dynamic_index_in_dim(send_rows[0], stretch_no, 0, keepdims=False)
        boundary_counts = lax.dynamic_index_in_dim(send_count[0], stretch_no, 0, keepdims=False)
        slot_marks = slot_ids[None, :] < boundary_counts[:, None]
        fetched = jnp.where(slot_marks[:, :, None], rows_in[row_picks], jnp.zeros((), jnp.bfloat16))
        fetched, slot_marks = (fetched, slot_marks.astype(jnp.bfloat16))
        halo_in, marks_in = (
            lax.all_to_all(fetched, "dom", split_axis=0, concat_axis=0, tiled=True),
            lax.all_to_all(slot_marks, "dom", split_axis=0, concat_axis=0, tiled=True),
        )
        aggregate_source_table = source_table
        aggregate_valid_rows = valid_rows
        halo_start = nodes_dev + stretch_no * halo_rows
        aggregate_source_table = put_rows(
            aggregate_source_table, halo_in.reshape(halo_rows, model_width), halo_start, active
        )
        aggregate_valid_rows = put_rows(
            aggregate_valid_rows,
            marks_in.reshape(halo_rows).astype(jnp.float32),
            halo_start,
            active,
        )
        counts = tile_count[0][stretch_no]
        sources = tile_src[0][stretch_no]
        targets = tile_dst[0][stretch_no]
        weights = tile_vals[0][stretch_no]
        live = tile_ids < counts
        picks = ((targets[:, None] == block_ids[None, :]) & live[:, None]).astype(jnp.bfloat16)
        placed = jnp.einsum("tr,tij->ritj", picks, weights, preferred_element_type=jnp.float32)
        dense = placed.astype(jnp.bfloat16).reshape(stretch_rows, tile_total * tile_size)
        gathered = jnp.concatenate(
            [
                lax.dynamic_slice_in_dim(
                    aggregate_source_table, sources[t] * tile_size, tile_size, 0
                )
                for t in range(tile_total)
            ],
            axis=0,
        )
        marks = (
            aggregate_valid_rows.reshape(-1, tile_size)[sources]
            .reshape(tile_total * tile_size)
            .astype(jnp.bfloat16)
        )
        add_summed = jnp.dot(dense, gathered, preferred_element_type=jnp.float32)
        add_degree = jnp.dot(dense, marks, preferred_element_type=jnp.float32)
        source_table = aggregate_source_table
        valid_rows = aggregate_valid_rows
        neighbour = (
            (rows_in.astype(jnp.float32) + add_summed) / (1.0 + add_degree)[:, None]
        ).astype(jnp.bfloat16)
        pre_norm = jnp.dot(rows_in, w_self[0], preferred_element_type=jnp.float32)
        pre_norm = (
            pre_norm
            + jnp.dot(neighbour, w_neigh[0], preferred_element_type=jnp.float32)
            + biases[0]
        )
        normed = (
            gains[0]
            * pre_norm
            * lax.rsqrt(jnp.mean(pre_norm * pre_norm, axis=-1, keepdims=True) + 1e-05)
        )
        previous = jnp.where(is_final, normed, jnp.maximum(normed, 0.0)).astype(jnp.bfloat16)
        outputs = put_rows(outputs, previous, stretch_no * stretch_rows, active)
    return outputs[None]


def layers_kernel(
    stretches,
    feat,
    w_self_hbm,
    w_neigh_hbm,
    bias_hbm,
    gain_hbm,
    listed_hbm,
    counts_hbm,
    dst_hbm,
    src_hbm,
    used_hbm,
    vals_hbm,
    out,
    h,
    staged,
    shared,
    share_out,
    halo_out,
    halo_in,
    marks_out,
    marks_in,
    vals,
    adj,
    picks,
    scales,
    sums,
    z,
    w_self,
    w_neigh,
    bias,
    gain,
    listed,
    counts,
    dst,
    src,
    used,
    h_sem,
    hop_sem,
    halo_send,
    halo_recv,
    share_sem,
    share_send,
    mark_send,
    mark_recv,
    vals_sem,
    w_sem,
    small_sem,
):
    pipes, peers = lax.axis_size("pipe"), lax.axis_size("dom")
    pipe, me = lax.axis_index("pipe"), lax.axis_index("dom")
    _, nodes, part = h.shape
    ch = nodes // stretches
    per_peer = halo_in.shape[3]
    halo = peers * per_peer
    tiles, tile = vals.shape[1:3]
    row_blocks = ch // tile
    pair = GROUP * part

    def rows(c):
        return pl.ds(c * ch, ch)

    def cols(j):
        return pl.ds(j * part, part)

    def arrived(ref, sem):
        pltpu.make_async_copy(ref, ref, sem).wait()

    def dot(a, b):
        return jnp.dot(a, b, preferred_element_type=jnp.float32)

    barrier = pltpu.get_barrier_semaphore()
    everyone = pipes * peers

    def greet(k, carry):
        other = lax.rem(pipe * peers + me + k, everyone)
        pl.semaphore_signal(
            barrier, inc=1, device_id=(other // peers, lax.rem(other, peers)), device_id_type=MESH
        )
        return carry

    def greet_peers():
        def one(k, carry):
            pl.semaphore_signal(
                barrier, inc=1, device_id=(pipe, lax.rem(me + k, peers)), device_id_type=MESH
            )
            return carry

        lax.fori_loop(1, peers, one, 0)
        pl.semaphore_signal(barrier, inc=1, device_id=(pipe - 1, me), device_id_type=MESH)

    @pl.when(pipe == 0)
    def _():
        lax.fori_loop(1, everyone, greet, 0)

    @pl.when(pipe > 0)
    def _():
        greet_peers()

    mine = pl.ds(pl.multiple_of(pipe * part, part), part)
    small = [
        pltpu.make_async_copy(listed_hbm, listed, small_sem.at[0]),
        pltpu.make_async_copy(counts_hbm, counts, small_sem.at[1]),
        pltpu.make_async_copy(dst_hbm, dst, small_sem.at[2]),
        pltpu.make_async_copy(src_hbm, src, small_sem.at[3]),
        pltpu.make_async_copy(used_hbm, used, small_sem.at[4]),
        pltpu.make_async_copy(bias_hbm, bias, small_sem.at[5]),
        pltpu.make_async_copy(gain_hbm, gain, small_sem.at[6]),
    ]
    share_loads = [
        pltpu.make_async_copy(feat.at[rows(c), mine], shared.at[rows(c)], share_sem.at[c])
        for c in range(stretches)
    ]
    tile_loads = [
        pltpu.make_async_copy(vals_hbm.at[0, c], vals.at[c], vals_sem.at[c])
        for c in range(stretches)
    ]
    weights = [
        pltpu.make_async_copy(w_self_hbm.at[0], w_self, w_sem.at[0]),
        pltpu.make_async_copy(w_neigh_hbm.at[0], w_neigh, w_sem.at[1]),
    ]
    for copy in small[:2] + share_loads[:1] + small[2:] + tile_loads[:1]:
        copy.start()

    @pl.when(pipe == 0)
    def _():
        for c in range(stretches):
            for j in range(CHUNKS):
                pltpu.make_async_copy(
                    feat.at[rows(c), cols(j)], h.at[j, rows(c)], h_sem.at[c, j]
                ).start()

    for copy in weights + share_loads[1:] + tile_loads[1:]:
        copy.start()

    small[0].wait()
    small[1].wait()

    slot = lax.broadcasted_iota(jnp.int32, (1, halo), 1)
    row_ids = lax.broadcasted_iota(jnp.int32, (halo, ch), 1)

    def make_pick(c):
        limit = jnp.zeros((1, halo), jnp.int32)
        for p in range(peers):
            limit = jnp.where(slot >= p * per_peer, p * per_peer + counts[0, c, p], limit)
        rows_listed = jnp.concatenate([listed[0, c, p : p + 1, :] for p in range(peers)], axis=1)
        wanted = jnp.where(slot < limit, rows_listed, -1).astype(jnp.float32)
        column = jnp.transpose(jnp.broadcast_to(wanted, (8, halo)))[:, :1].astype(jnp.int32)
        picks[c] = jnp.where(row_ids == column, 1.0, 0.0).astype(jnp.bfloat16)

    def share(c):
        share_loads[c].wait()
        sent = dot(picks[c], shared[rows(c), :])
        share_out[c] = sent.astype(jnp.bfloat16).reshape(peers, per_peer, part)

        def send(k, carry):
            down = peers - k - jnp.where(peers - k <= me, 1, 0)
            up = k - 1 + jnp.where(k - 1 >= me, 1, 0)
            to = jnp.where(k == 0, me, jnp.where(me < peers // 2, down, up))
            pltpu.make_async_remote_copy(
                src_ref=share_out.at[c, to],
                dst_ref=halo_in.at[c, pipe, me],
                send_sem=share_send.at[c],
                recv_sem=halo_recv.at[c, pipe],
                device_id=(0, to),
                device_id_type=MESH,
            ).start()
            return carry

        def fan_out():
            lax.fori_loop(1, peers, send, 0)

            @pl.when(pipe == 0)
            def _():
                pltpu.make_async_copy(
                    share_out.at[c, me], halo_in.at[c, 0, me], halo_recv.at[c, 0]
                ).start()

            @pl.when(pipe > 0)
            def _():
                send(0, 0)

        if c == 0:
            fan_out()
        else:
            pl.when(pipe != 1)(fan_out)

            @pl.when(pipe == 0)
            def _():
                send_picked(c, 1)

    make_pick(0)

    later = jnp.where(pipe < pipes - 1, 2 * peers, 2 * peers - 1)
    pl.semaphore_wait(barrier, jnp.where(pipe == 0, peers, later))
    share(0)

    mark_shape = marks_out.shape[1:]
    mark_row = lax.broadcasted_iota(jnp.int32, mark_shape, 0)
    mark_slot = lax.broadcasted_iota(jnp.int32, mark_shape, 1) - me * per_peer
    for p in range(peers):
        limit = jnp.zeros(mark_shape, jnp.int32)
        for c in range(stretches):
            limit = jnp.where(mark_row == c, counts[0, c, p], limit)
        mark = (mark_slot >= 0) & (mark_slot < limit)
        marks_out[p] = jnp.where(mark, 1.0, 0.0).astype(jnp.bfloat16)

    def send_marks(k, carry):
        to = lax.rem(me + k, peers)
        pltpu.make_async_remote_copy(
            src_ref=marks_out.at[to],
            dst_ref=marks_in.at[me],
            send_sem=mark_send,
            recv_sem=mark_recv,
            device_id=(pipe, to),
            device_id_type=MESH,
        ).start()
        return carry

    lax.fori_loop(1, peers, send_marks, 0)
    pltpu.make_async_copy(marks_out.at[me], marks_in.at[me], mark_recv).start()

    for copy in small[2:5]:
        copy.wait()

    def build(c):
        tile_loads[c].wait()
        codes = [
            jnp.where(t < used[0, c], src[0, c, t] * row_blocks + dst[0, c, t], -1)
            for t in range(tiles)
        ]

        def blocks(first, count):
            def one(i, carry):
                b = first + i
                totals = [jnp.zeros((tile, tile), jnp.float32) for _ in range(row_blocks)]
                for t in range(tiles):
                    weight = vals[c, t].astype(jnp.float32)
                    for r in range(row_blocks):
                        on = jnp.where(codes[t] == b * row_blocks + r, 1.0, 0.0)
                        totals[r] = totals[r] + weight * on
                at = pl.ds(pl.multiple_of(b * tile, tile), tile)
                for r in range(row_blocks):
                    adj[c, r * tile : (r + 1) * tile, at] = totals[r].astype(jnp.bfloat16)
                return carry

            lax.fori_loop(0, count, one, 0)

        blocks(0, (c + 1) * ch // tile)
        blocks(nodes // tile, (c + 1) * halo // tile)

    over_rows = (((1,), (1,)), ((), ()))

    def far(c, d):
        return adj[c, :, nodes + d * halo : nodes + (d + 1) * halo]

    def make_scale(c):
        own = (c + 1) * ch
        valid = marks_in[0]
        for q in range(1, peers):
            valid = valid + marks_in[q]
        ones = jnp.ones((valid.shape[0], own), jnp.bfloat16)
        deg = lax.dot_general(
            adj[c, :, :own], ones, over_rows, preferred_element_type=jnp.float32
        )[:, :1]
        for d in range(c + 1):
            deg = deg + lax.dot_general(
                far(c, d), valid, over_rows, preferred_element_type=jnp.float32
            )[:, d : d + 1]
        scales[c] = jnp.broadcast_to(1.0 / (1.0 + deg), (ch, part))

    def send_chunk(c, j):
        arrived(h.at[j, rows(c)], h_sem.at[c, j])
        send_picked(c, j)

    def send_picked(c, j):
        sent = dot(picks[c], h[j, rows(c), :])
        halo_out[c, j] = sent.astype(jnp.bfloat16).reshape(peers, per_peer, part)

        def send(k, carry):
            down = peers - k - jnp.where(peers - k <= me, 1, 0)
            up = k - 1 + jnp.where(k - 1 >= me, 1, 0)
            to = jnp.where(me < peers // 2, down, up)
            pltpu.make_async_remote_copy(
                src_ref=halo_out.at[c, j, to],
                dst_ref=halo_in.at[c, j, me],
                send_sem=halo_send.at[c, j],
                recv_sem=halo_recv.at[c, j],
                device_id=(pipe, to),
                device_id_type=MESH,
            ).start()
            return carry

        lax.fori_loop(1, peers, send, 0)
        pltpu.make_async_copy(
            halo_out.at[c, j, me], halo_in.at[c, j, me], halo_recv.at[c, j]
        ).start()

    def near_sums(c, js):
        own = (c + 1) * ch
        span = pl.ds(js[0] * part, len(js) * part)
        held = jnp.concatenate([h[j, rows(c), :] for j in js], axis=1)
        before = bias[...] if js[0] == 0 else z[...]
        z[...] = before + dot(held, w_self[span, :])
        added = held.astype(jnp.float32) + dot(
            adj[c, :, :own], jnp.concatenate([h[j, :own, :] for j in js], axis=1)
        )
        for d in range(c):
            added = added + dot(
                far(c, d), jnp.concatenate([halo_in[d, j].reshape(halo, part) for j in js], axis=1)
            )
        sums[:, span] = added

    def far_sums(c, js):
        for j in js:
            arrived(halo_in.at[c, j], halo_recv.at[c, j])
        fetched = jnp.concatenate([halo_in[c, j].reshape(halo, part) for j in js], axis=1)
        span = pl.ds(js[0] * part, len(js) * part)
        scale = jnp.concatenate([scales[c]] * len(js), axis=1)
        agg = (sums[:, span] + dot(far(c, c), fetched)) * scale
        z[...] += dot(agg.astype(jnp.bfloat16), w_neigh[span, :])

    floor = jnp.where(pipe == pipes - 1, -jnp.inf, 0.0).astype(jnp.float32)

    def finish(c):
        value = z[...]
        u = gain[...] * value * lax.rsqrt(jnp.mean(value * value, axis=-1, keepdims=True) + 1e-05)
        result = jnp.maximum(u, floor).astype(jnp.bfloat16)

        def hop(j):
            staged[j, rows(c), :] = result[:, j * part : (j + 1) * part]
            pltpu.make_async_remote_copy(
                src_ref=staged.at[j, rows(c)],
                dst_ref=h.at[j, rows(c)],
                send_sem=hop_sem.at[c, j],
                recv_sem=h_sem.at[c, j],
                device_id=(pipe + 1, me),
                device_id_type=MESH,
            ).start()

        @pl.when(pipe < pipes - 1)
        def _():
            for j in range(CHUNKS):
                hop(j)

        out[rows(c), :] = result

    def wait_weights():
        for copy in weights + small[5:]:
            copy.wait()

    build(0)

    @pl.when(pipe == 0)
    def _():
        for c in range(stretches):
            if c == 0:
                for d in range(stretches):
                    for j in range(CHUNKS):
                        arrived(h.at[j, rows(d)], h_sem.at[d, j])
                wait_weights()
            near_sums(c, (0, 1))
            near_sums(c, (2, 3))
            if c == 0:
                make_pick(1)
                share(1)
                arrived(marks_in, mark_recv)
            make_scale(c)
            for j in range(CHUNKS):
                far_sums(c, (j,))
            finish(c)
            if c + 2 < stretches:
                make_pick(c + 2)
                share(c + 2)
            if c + 1 < stretches:
                build(c + 1)

    @pl.when(pipe > 0)
    def _():
        build(1)
        build(2)
        make_pick(1)
        share(1)
        build(3)
        make_pick(2)
        share(2)
        arrived(marks_in, mark_recv)
        for c in range(stretches):
            make_scale(c)
        wait_weights()
        make_pick(3)
        share(3)
        for j in range(CHUNKS):
            send_chunk(0, j)
        for c in range(stretches):
            near_sums(c, (0, 1))
            near_sums(c, (2, 3))
            for j in range(CHUNKS):
                if c + 1 < stretches and CHUNKS - j <= LEAD:
                    send_chunk(c + 1, j + LEAD - CHUNKS)
                far_sums(c, (j,))
            finish(c)
            if c + 1 < stretches:
                for j in range(LEAD, CHUNKS):
                    send_chunk(c + 1, j)

    others = pl.ds(0, peers - 1)
    arrived(marks_out.at[others], mark_send)

    @pl.when(pipe == 0)
    def _():
        for c in range(stretches):
            arrived(share_out.at[c, others], share_send.at[c])
            if c > 0:
                arrived(halo_out.at[c, 1, others], halo_send.at[c, 1])

    @pl.when(pipe > 0)
    def _():
        for c in range(stretches):
            if c == 0:
                arrived(share_out.at[c], share_send.at[c])
            else:

                @pl.when(pipe > 1)
                def _():
                    arrived(share_out.at[c], share_send.at[c])

            for j in range(CHUNKS):
                arrived(halo_out.at[c, j, others], halo_send.at[c, j])

    @pl.when(pipe < pipes - 1)
    def _():
        for c in range(stretches):
            for j in range(CHUNKS):
                arrived(staged.at[j, rows(c)], hop_sem.at[c, j])


def pipelined(
    features,
    w_self,
    w_neigh,
    biases,
    gains,
    send_rows,
    send_count,
    tile_dst,
    tile_src,
    tile_count,
    tile_vals,
):
    peers = lax.axis_size("dom")
    nodes, width = features.shape
    stretches = tile_count.shape[1]
    per_peer = send_rows.shape[3]
    ch = nodes // stretches
    halo = peers * per_peer
    part = width // CHUNKS
    sources = nodes + stretches * halo
    tiles = tile_vals.shape[1:]
    anywhere = pl.BlockSpec(memory_space=pltpu.HBM)
    halo_shape = (stretches, CHUNKS, peers, per_peer, part)
    out = pl.pallas_call(
        functools.partial(layers_kernel, stretches),
        out_shape=pltpu.VMEM((nodes, width), jnp.bfloat16),
        in_specs=[anywhere] * 11,
        out_specs=pl.BlockSpec(memory_space=pltpu.VMEM),
        scratch_shapes=[
            pltpu.VMEM((CHUNKS, nodes, part), jnp.bfloat16),
            pltpu.VMEM((CHUNKS, nodes, part), jnp.bfloat16),
            pltpu.VMEM((nodes, part), jnp.bfloat16),
            pltpu.VMEM((stretches, peers, per_peer, part), jnp.bfloat16),
            pltpu.VMEM(halo_shape, jnp.bfloat16),
            pltpu.VMEM(halo_shape, jnp.bfloat16),
            pltpu.VMEM((peers, 8, halo), jnp.bfloat16),
            pltpu.VMEM((peers, 8, halo), jnp.bfloat16),
            pltpu.VMEM(tiles, jnp.bfloat16),
            pltpu.VMEM((stretches, ch, sources), jnp.bfloat16),
            pltpu.VMEM((stretches, halo, ch), jnp.bfloat16),
            pltpu.VMEM((stretches, ch, part), jnp.float32),
            pltpu.VMEM((ch, width), jnp.float32),
            pltpu.VMEM((ch, width), jnp.float32),
            pltpu.VMEM((width, width), jnp.bfloat16),
            pltpu.VMEM((width, width), jnp.bfloat16),
            pltpu.VMEM(biases.shape, jnp.float32),
            pltpu.VMEM(gains.shape, jnp.float32),
            pltpu.VMEM(send_rows.shape, jnp.int32),
            pltpu.SMEM(send_count.shape, jnp.int32),
            pltpu.SMEM(tile_dst.shape, jnp.int32),
            pltpu.SMEM(tile_src.shape, jnp.int32),
            pltpu.SMEM(tile_count.shape, jnp.int32),
            pltpu.SemaphoreType.DMA((stretches, CHUNKS)),
            pltpu.SemaphoreType.DMA((stretches, CHUNKS)),
            pltpu.SemaphoreType.DMA((stretches, CHUNKS)),
            pltpu.SemaphoreType.DMA((stretches, CHUNKS)),
            pltpu.SemaphoreType.DMA((stretches,)),
            pltpu.SemaphoreType.DMA((stretches,)),
            pltpu.SemaphoreType.DMA,
            pltpu.SemaphoreType.DMA,
            pltpu.SemaphoreType.DMA((stretches,)),
            pltpu.SemaphoreType.DMA((2,)),
            pltpu.SemaphoreType.DMA((7,)),
        ],
        compiler_params=pltpu.CompilerParams(
            collective_id=0, has_side_effects=True, vmem_limit_bytes=40 * 2**20
        ),
        name="layers",
    )(
        *(
            pltpu.with_memory_space_constraint(array, pltpu.HBM)
            for array in (
                features,
                w_self,
                w_neigh,
                biases,
                gains,
                send_rows,
                send_count,
                tile_dst,
                tile_src,
                tile_count,
                tile_vals,
            )
        )
    )
    return out[None]


def on_device(*args):
    send_rows, tile_vals = args[5], args[10]
    per_peer, tile = send_rows.shape[3], tile_vals.shape[-1]
    if per_peer % 16 or tile != 128 or args[9].shape[1] > 8 or lax.axis_size("pipe") != CHUNKS:
        return staged_exchange(*args)
    return pipelined(*args)


def solution(mesh):
    placed = (
        P("dom", None),
        P("pipe", None, None),
        P("pipe", None, None),
        P("pipe", None),
        P("pipe", None),
        P("dom", None, None, None),
        P("dom", None, None),
        P("dom", None, None),
        P("dom", None, None),
        P("dom", None),
        P("dom", None, None, None, None),
    )
    return jax.shard_map(
        on_device, mesh=mesh, in_specs=placed, out_specs=P("pipe", "dom", None), check_vma=False
    )
```
